512 devices in a mesh: tm: 32 (over y, x), chan: 16 (over z, core).
Axes of the slice: x: 4, y: 8, z: 8, core: 2. Of those that a mesh axis runs over, the one named last changes fastest.
Arguments:
- record: bfloat16 [32768, 10240], P('tm', 'chan'), may hold values from -6 to 6
- fir_taps: bfloat16 [64], replicated, may hold values from -0.75 to 0.75
- gauge_lag: int32 [10240], P('chan'), may hold values from 1 to 16
- projector: bfloat16 [32768, 128], P('tm'), may hold values from -0.1875 to 0.1875
- compress: float32 [256, 128], replicated, may hold values from -0.5 to 0.5
Outputs:
- sketch: float32 [128, 10240], P('tm', 'chan')
The draws below stay inside these ranges and needn't reach their ends.
Inputs may be any that keep to these rules, and one draw needn't show every extreme that they name: `gauge_lag`: some channel has lag 16.
All inputs are finite; a program needn't handle non-finite values.
Results may differ from the reference program's by a relative error of at most 0.0028.
Values may be sent and summed in bfloat16 or wider, within the bound.
A program may use at most 64 MiB of HBM per device.

```python
import jax
import jax.numpy as jnp
from jax import lax

CHANNELS = 10240
RANK = 128
TAPS = 64
GAUGE_MAX = 16
K_ITERS = 8
S_DEV = 1024
TIME = 32768
LEVELS = 5
N_TM = 32


def plant(drawn, rng, least, high):
    longest = drawn.shape.index(max(drawn.shape))
    spots = []
    for shift in (0, 1):
        where = [jax.random.randint(jax.random.fold_in(rng, axis), (), 0, length) for axis, length in enumerate(drawn.shape)]
        where[longest] = (where[longest] + shift) % drawn.shape[longest]
        spots.append(tuple(where))
    return drawn.at[spots[0]].set(least).at[spots[1]].set(high)


def steps_of(stream_key, extent, shards, low, top_value):
    def one(dim, blocks):
        draws = jax.random.uniform(jax.random.fold_in(jax.random.fold_in(stream_key, 6), dim), (blocks,), jnp.float32, low / len(shards), top_value / len(shards))
        return jnp.repeat(jnp.exp(draws), extent[dim] // blocks).reshape((-1,) + (1,) * (len(extent) - dim - 1))

    level = one(*shards[0])
    for cut in shards[1:]:
        level = level * one(*cut)
    return level


def centred(stream_key, shape, scale, most, shards=(), kind=jnp.bfloat16):
    level = steps_of(stream_key, shape, shards, -0.22, 0.18) if shards else 1.0
    values = jax.random.normal(stream_key, shape, jnp.float32) * scale * level
    return jnp.minimum(jnp.maximum(values, -most), most).astype(kind)


def setup_inputs(seed: int = 0) -> dict:
    streams_of = jax.random.split(jax.random.key(seed), 6)
    return {
        "record": centred(streams_of[0], (TIME, CHANNELS), 1.0, 6.0, ((0, 32), (1, 16))),
        "fir_taps": centred(streams_of[1], (TAPS,), TAPS ** -0.5, 0.75),
        "gauge_lag": plant(jax.random.randint(streams_of[2], (CHANNELS,), 1, GAUGE_MAX + 1), jax.random.fold_in(streams_of[2], 1), 1, GAUGE_MAX).astype(jnp.int32),
        "projector": centred(streams_of[3], (TIME, RANK), S_DEV ** -0.5, 0.1875, ((0, 32),)),
        "compress": centred(streams_of[4], (2 * RANK, RANK), RANK ** -0.5, 0.5, (), jnp.float32),
    }


def merge_pair(stacked, compress):
    width = stacked.shape[0]
    eye = jnp.eye(width, dtype=jnp.float32)
    gram = jnp.dot(stacked, stacked.T, precision=lax.Precision.HIGHEST, preferred_element_type=jnp.float32)
    mean_level = jnp.trace(gram) / width
    shifted = gram - mean_level * eye
    signed = shifted / jnp.sqrt(jnp.sum(shifted * shifted) + 1e-06)
    for step_index in range(K_ITERS):
        square = jnp.dot(signed, signed, precision=lax.Precision.HIGHEST, preferred_element_type=jnp.float32)
        signed = jnp.dot(signed, 1.5 * eye - 0.5 * square, precision=lax.Precision.HIGHEST, preferred_element_type=jnp.float32)
    filter_mat = 0.5 * (eye + signed)
    mixing = jnp.dot(compress.T, filter_mat, precision=lax.Precision.HIGHEST, preferred_element_type=jnp.float32)
    return jnp.dot(mixing, stacked, precision=lax.Precision.HIGHEST, preferred_element_type=jnp.float32)

def reference(record, fir_taps, gauge_lag, projector, compress):
    halo_rows = TAPS - 1 + GAUGE_MAX
    padded = jnp.concatenate([jnp.zeros((halo_rows, CHANNELS), jnp.bfloat16), record], 0)
    taps_wide = fir_taps.astype(jnp.float32)

    def one_block(block_index):
        start = (block_index * S_DEV).astype(jnp.int32)
        extended = lax.dynamic_slice(padded, (start, jnp.int32(0)), (S_DEV + halo_rows, CHANNELS)).astype(jnp.float32)
        filtered = jnp.zeros((S_DEV + GAUGE_MAX, CHANNELS), jnp.float32)
        for tap_index in range(TAPS):
            first = TAPS - 1 - tap_index
            filtered = filtered + taps_wide[tap_index] * extended[first:first + S_DEV + GAUGE_MAX]
        current = filtered[GAUGE_MAX:]
        lagged = jnp.zeros((S_DEV, CHANNELS), jnp.float32)
        for lag_step in range(1, GAUGE_MAX + 1):
            chosen = (gauge_lag == lag_step).astype(jnp.float32)[None, :]
            lagged = lagged + chosen * filtered[GAUGE_MAX - lag_step:GAUGE_MAX - lag_step + S_DEV]
        strain = (current - lagged).astype(jnp.bfloat16)
        block_proj = lax.dynamic_slice(projector, (start, jnp.int32(0)), (S_DEV, RANK))
        return jnp.dot(block_proj.T, strain, preferred_element_type=jnp.float32)
    sketches = lax.map(one_block, jnp.arange(N_TM, dtype=jnp.int32))
    for depth_level in range(LEVELS):
        count_now = sketches.shape[0]
        pairs = sketches.reshape(count_now // 2, 2 * RANK, CHANNELS)
        sketches = lax.map(lambda stacked: merge_pair(stacked, compress), pairs)
    return sketches[0]
```

```python
import functools

import jax
import jax.numpy as jnp
from jax import lax
from jax.experimental import pallas as pl
from jax.experimental.pallas import tpu as pltpu
from jax.sharding import PartitionSpec as P

TAPS = 64
GAUGE_MAX = 16
K_ITERS = 8
HALO = 80
RANK = 128
BLOCK = 128
MESH = pl.DeviceIdType.MESH
F32 = jnp.float32
BF16 = jnp.bfloat16


def split(value):
    high = value.astype(BF16)
    return high, (value - high.astype(F32)).astype(BF16)


def dot(first, second, contract=((1,), (0,))):
    return lax.dot_general(first, second, (contract, ((), ())), preferred_element_type=F32)


def dot3(first, second, contract=((1,), (0,))):
    fh, fl = first
    sh, sl = second
    return dot(fh, sh, contract) + (dot(fh, sl, contract) + dot(fl, sh, contract))


NT = ((1,), (1,))
TN = ((0,), (0,))


def kernel(n_tm, n_chan, levels, record, base_ref, lag_ref, proj_ref, comp_ref, out_ref,
           ext, filtered, strain, stk, stk_hi, stk_lo, gram, diag, comp_t, part, scat, gath,
           z_ref, a_ref, b_ref, local_sem, halo_sem, ex_sem, dg_sem, rs_send, rs_recv, ag_send, ag_recv):
    tm = lax.axis_index("tm")
    me = lax.axis_index("chan")
    n_rows, n_cols = record.shape
    slice_rows = RANK // n_chan
    n_blocks = n_rows // BLOCK
    n_tiles = n_cols // 128

    load = pltpu.make_async_copy(record, ext.at[pl.ds(HALO, n_rows)], local_sem)
    load.start()

    nxt = lax.rem(tm + 1, n_tm)
    prv = lax.rem(tm + n_tm - 1, n_tm)
    partners = []
    for level in range(levels):
        bit = 2**level
        partners.append(tm + bit * (1 - 2 * lax.rem(tm // bit, 2)))
    offsets = sorted(range(1, n_chan), key=lambda o: -min(o, n_chan - o))

    barrier = pltpu.get_barrier_semaphore()
    for who in [nxt, prv] + partners:
        pl.semaphore_signal(barrier, inc=1, device_id={"tm": who}, device_id_type=MESH)
    for o in offsets:
        pl.semaphore_signal(barrier, inc=1, device_id={"chan": lax.rem(me + o, n_chan)}, device_id_type=MESH)
    pl.semaphore_wait(barrier, 2 + levels + n_chan - 1)

    halo = pltpu.make_async_remote_copy(
        src_ref=record.at[pl.ds(n_rows - HALO, HALO)], dst_ref=ext.at[pl.ds(0, HALO)],
        send_sem=halo_sem.at[0], recv_sem=halo_sem.at[1], device_id={"tm": nxt}, device_id_type=MESH)
    halo.start()

    toeplitz = pltpu.roll(jnp.broadcast_to(base_ref[...], (BLOCK, 256)), 0, 1, stride=1, stride_axis=0)
    toeplitz = toeplitz[:, :BLOCK + TAPS].astype(BF16)
    comp = comp_ref[...].T
    comp_t[0] = comp
    comp_t[1, :, 0:RANK] = comp[:, RANK:]
    comp_t[1, :, RANK:] = comp[:, :RANK]
    load.wait()

    def fir(block):
        start = pl.multiple_of(block * BLOCK, BLOCK)
        window = ext[pl.ds(start + GAUGE_MAX, BLOCK + TAPS)]
        filtered[pl.ds(start + GAUGE_MAX, BLOCK)] = dot(toeplitz, window)

    @pl.loop(1, n_blocks)
    def _(block):
        fir(block)

    halo.wait()
    ext[pl.ds(0, HALO)] = jnp.where(tm == 0, jnp.zeros((HALO, n_cols), BF16), ext[pl.ds(0, HALO)])
    filtered[pl.ds(0, GAUGE_MAX)] = dot(toeplitz[:GAUGE_MAX, :HALO], ext[pl.ds(0, HALO)])
    fir(jnp.int32(0))

    rows = BLOCK + GAUGE_MAX
    masks = []
    for tile in range(n_tiles):
        lag = lag_ref[:, tile * 128:(tile + 1) * 128] - 1
        masks.append([lax.rem(lag // (2**b), 2) == 1 for b in range(4)])

    @pl.loop(0, n_blocks)
    def _(block):
        start = pl.multiple_of(block * BLOCK, BLOCK)
        for tile in range(n_tiles):
            cols = slice(tile * 128, (tile + 1) * 128)
            x = filtered[pl.ds(start, rows), cols]
            y = pltpu.roll(x, 1, 0)
            for b in (3, 2, 1, 0):
                y = jnp.where(jnp.broadcast_to(masks[tile][b], (rows, 128)), pltpu.roll(y, 2**b, 0), y)
            strain[pl.ds(start, BLOCK), cols] = (x - y)[GAUGE_MAX:].astype(BF16)

    stk[0, 0:RANK] = dot(proj_ref[...], strain[...], TN)

    def exchange(level):
        copy = pltpu.make_async_remote_copy(
            src_ref=stk.at[level, pl.ds(0, RANK)], dst_ref=stk.at[level, pl.ds(RANK, RANK)],
            send_sem=ex_sem.at[0, level], recv_sem=ex_sem.at[1, level],
            device_id={"tm": partners[level]}, device_id_type=MESH)
        copy.start()
        return copy

    def send_diag(level):
        copy = pltpu.make_async_remote_copy(
            src_ref=diag.at[level, 0], dst_ref=diag.at[level, 1],
            send_sem=dg_sem.at[0, level], recv_sem=dg_sem.at[1, level],
            device_id={"tm": partners[level]}, device_id_type=MESH)
        copy.start()
        return copy

    def scatter(j, value):
        value = value.reshape(n_chan, slice_rows, RANK)
        part[j] = value
        scat[j, me] = part[j, me]
        copies = []
        for o in offsets:
            peer = lax.rem(me + o, n_chan)
            copy = pltpu.make_async_remote_copy(
                src_ref=part.at[j, peer], dst_ref=scat.at[j, me],
                send_sem=rs_send.at[j, o], recv_sem=rs_recv.at[j, o],
                device_id={"chan": peer}, device_id_type=MESH)
            copy.start()
            copies.append(copy)
        return copies

    def gather(j, copies):
        for copy in copies:
            copy.wait()
        gath[j, me] = jnp.sum(scat[j], axis=0)
        copies = []
        for o in offsets:
            peer = lax.rem(me + o, n_chan)
            copy = pltpu.make_async_remote_copy(
                src_ref=gath.at[j, me], dst_ref=gath.at[j, me],
                send_sem=ag_send.at[j, o], recv_sem=ag_recv.at[j, o],
                device_id={"chan": peer}, device_id_type=MESH)
            copy.start()
            copies.append(copy)
        return copies

    def finish(j, copies):
        for copy in copies:
            copy.wait()
        return gath[j].reshape(RANK, RANK)

    eye = (lax.broadcasted_iota(jnp.int32, (2 * RANK, 2 * RANK), 0)
           == lax.broadcasted_iota(jnp.int32, (2 * RANK, 2 * RANK), 1)).astype(F32)

    def split_rows(level, low):
        high, rest = split(stk[level, low:low + RANK])
        stk_hi[low:low + RANK] = high
        stk_lo[low:low + RANK] = rest
        return high, rest

    diag_copy = None
    for level in range(levels):
        moving = exchange(level)
        own = split_rows(level, 0)
        if level == 0:
            diag_moving = scatter(levels, dot3(own, own, NT))
        else:
            mix, whole = split(a_ref_mix), split(gram[...])
            diag[level, 0] = dot3(split(dot3(mix, whole)), mix, NT)
            diag_copy = send_diag(level)
        moving.wait()
        other = split_rows(level, RANK)
        cross_moving = scatter(level, dot3(own, other, NT))
        if level == 0:
            diag_moving = gather(levels, diag_moving)
        cross_moving = gather(level, cross_moving)
        if level == 0:
            diag[level, 0] = finish(levels, diag_moving)
            diag_copy = send_diag(level)
        cross = finish(level, cross_moving)
        gram[0:RANK, RANK:] = cross
        gram[RANK:, 0:RANK] = cross.T
        gram[0:RANK, 0:RANK] = diag[level, 0]
        diag_copy.wait()
        gram[RANK:, RANK:] = diag[level, 1]

        value = gram[...]
        mean = jnp.sum(value * eye, keepdims=True) / (2 * RANK)
        shifted = value - mean * eye
        z_ref[...] = shifted / jnp.sqrt(jnp.sum(shifted * shifted, keepdims=True) + 1e-06)

        @pl.loop(0, K_ITERS)
        def _(step):
            z = split(z_ref[...])
            poly = 1.5 * eye - 0.5 * dot3(z, z)
            z_ref[...] = dot3(z, split(poly))

        upper = lax.rem(tm // 2**level, 2)
        if level < levels - 1:
            mine = comp_t[upper]
            mix_value = 0.5 * (mine + dot3(split(mine), split(z_ref[...])))
            a_ref_mix = mix_value
            mix = split(mix_value)
            stk[level + 1, 0:RANK] = dot3(mix, (stk_hi[...], stk_lo[...]))
        else:
            share = RANK // n_tm
            group = max(8, share)
            start = pl.multiple_of(tm * share // group * group, 8)
            mine = comp_t[upper, pl.ds(start, group)]
            mix = split(0.5 * (mine + dot3(split(mine), split(z_ref[...]))))
            result = dot3(mix, (stk_hi[...], stk_lo[...]))
            place = lax.rem(tm, group // share)
            picked = result[0:share]
            for i in range(1, group // share):
                picked = jnp.where(place == i, result[i * share:(i + 1) * share], picked)
            out_ref[...] = picked


def on_device(n_tm, n_chan, record, fir_taps, gauge_lag, projector, compress):
    n_rows, n_cols = record.shape
    levels = n_tm.bit_length() - 1
    base = lax.pad(lax.rev(fir_taps.astype(F32), (0,)), jnp.float32(0), ((1, 255 - TAPS, 0),)).reshape(1, 256)
    lag = gauge_lag.reshape(1, n_cols)
    slice_rows = RANK // n_chan
    dma = pltpu.SemaphoreType.DMA
    vmem = pl.BlockSpec(memory_space=pltpu.VMEM)
    return pl.pallas_call(
        functools.partial(kernel, n_tm, n_chan, levels),
        out_shape=jax.ShapeDtypeStruct((RANK // n_tm, n_cols), F32),
        in_specs=[pl.BlockSpec(memory_space=pl.ANY), vmem, vmem, vmem, vmem],
        out_specs=vmem,
        scratch_shapes=[
            pltpu.VMEM((HALO + n_rows, n_cols), BF16),
            pltpu.VMEM((GAUGE_MAX + n_rows, n_cols), F32),
            pltpu.VMEM((n_rows, n_cols), BF16),
            pltpu.VMEM((levels, 2 * RANK, n_cols), F32),
            pltpu.VMEM((2 * RANK, n_cols), BF16),
            pltpu.VMEM((2 * RANK, n_cols), BF16),
            pltpu.VMEM((2 * RANK, 2 * RANK), F32),
            pltpu.VMEM((levels, 2, RANK, RANK), F32),
            pltpu.VMEM((2, RANK, 2 * RANK), F32),
            pltpu.VMEM((levels + 1, n_chan, slice_rows, RANK), F32),
            pltpu.VMEM((levels + 1, n_chan, slice_rows, RANK), F32),
            pltpu.VMEM((levels + 1, n_chan, slice_rows, RANK), F32),
            pltpu.VMEM((2 * RANK, 2 * RANK), F32),
            pltpu.VMEM((2 * RANK, 6 * RANK), BF16),
            pltpu.VMEM((6 * RANK, 2 * RANK), BF16),
            dma,
            dma((2,)),
            dma((2, levels)),
            dma((2, levels)),
            dma((levels + 1, n_chan)),
            dma((levels + 1, n_chan)),
            dma((levels + 1, n_chan)),
            dma((levels + 1, n_chan)),
        ],
        compiler_params=pltpu.CompilerParams(collective_id=0, has_side_effects=True, vmem_limit_bytes=40 * 2**20),
    )(record, base, lag, projector, compress)


def solution(mesh):
    return jax.shard_map(
        functools.partial(on_device, mesh.shape["tm"], mesh.shape["chan"]),
        mesh=mesh,
        in_specs=(P("tm", "chan"), P(), P("chan"), P("tm", None), P()),
        out_specs=P("tm", "chan"),
        check_vma=False,
    )
```

```python
import functools

import jax
import jax.numpy as jnp
from jax import lax
from jax.experimental import pallas as pl
from jax.experimental.pallas import tpu as pltpu
from jax.sharding import PartitionSpec as P

TAPS = 64
GAUGE_MAX = 16
K_ITERS = 8
HALO = 80
RANK = 128
BLOCK = 128
MOST = 8
MESH = pl.DeviceIdType.MESH
F32 = jnp.float32
BF16 = jnp.bfloat16


def split(value):
    high = value.astype(BF16)
    return high, (value - high.astype(F32)).astype(BF16)


def dot(first, second, contract=((1,), (0,))):
    return lax.dot_general(first, second, (contract, ((), ())), preferred_element_type=F32)


def dot3(first, second, contract=((1,), (0,))):
    fh, fl = first
    sh, sl = second
    return dot(fh, sh, contract) + (dot(fh, sl, contract) + dot(fl, sh, contract))


NT = ((1,), (1,))
TN = ((0,), (0,))


def kernel(n_tm, n_chan, levels, record, base_ref, lag_ref, proj_hbm, comp_hbm, out_ref,
           ext, filtered, strain, proj_ref, comp_ref, stk, stk_hi, stk_lo, gram, diag, comp_t, part, scat, gath,
           crossp, pre, zbuf, cross, give, take, mix_hi, mix_lo,
           local_sem, halo_sem, ex_sem, dg_sem, rs_send, rs_recv, ag_send, ag_recv,
           pre_sem, z_send, z_recv, g_send, g_recv, f_send, f_recv, last_sem):
    tm = lax.axis_index("tm")
    me = lax.axis_index("chan")
    n_rows, n_cols = record.shape
    slice_rows = RANK // n_chan
    n_blocks = n_rows // BLOCK
    n_tiles = n_cols // 128
    n_z = n_chan // 2
    core = lax.rem(me, 2)
    z_me = me // 2
    other_core = me + 1 - 2 * core

    load = pltpu.make_async_copy(record, ext.at[pl.ds(HALO, n_rows)], local_sem.at[0])
    load_proj = pltpu.make_async_copy(proj_hbm, proj_ref, local_sem.at[1])
    load_comp = pltpu.make_async_copy(comp_hbm, comp_ref, local_sem.at[2])
    load.start()
    load_proj.start()
    load_comp.start()

    nxt = lax.rem(tm + 1, n_tm)
    prv = lax.rem(tm + n_tm - 1, n_tm)
    partners = []
    for level in range(levels):
        bit = 2**level
        partners.append(tm + bit * (1 - 2 * lax.rem(tm // bit, 2)))
    offsets = sorted(range(1, n_chan), key=lambda o: -min(o, n_chan - o))
    z_offsets = sorted(range(1, n_z), key=lambda o: -min(o, n_z - o))
    most = min(MOST, n_tm)

    def member(count, i):
        return tm // count * count + lax.rem(tm + i, count)

    barrier = pltpu.get_barrier_semaphore()
    greeted = [{"tm": nxt}, {"tm": prv}]
    greeted += [{"tm": partners[level]} for level in range(levels) if 2**level >= most]
    greeted += [{"chan": lax.rem(me + o, n_chan)} for o in offsets]
    greeted += [{"tm": member(most, i), "chan": c} for i in range(1, most) for c in (me, other_core)]
    for who in greeted:
        pl.semaphore_signal(barrier, inc=1, device_id=who, device_id_type=MESH)
    pl.semaphore_wait(barrier, len(greeted))

    halo = pltpu.make_async_remote_copy(
        src_ref=record.at[pl.ds(n_rows - HALO, HALO)], dst_ref=ext.at[pl.ds(0, HALO)],
        send_sem=halo_sem.at[0], recv_sem=halo_sem.at[1], device_id={"tm": nxt}, device_id_type=MESH)
    halo.start()

    toeplitz = pltpu.roll(jnp.broadcast_to(base_ref[...], (BLOCK, 256)), 0, 1, stride=1, stride_axis=0)
    toeplitz = toeplitz[:, :BLOCK + TAPS].astype(BF16)
    load.wait()

    def fir(block):
        start = block * BLOCK
        window = ext[start + GAUGE_MAX:start + GAUGE_MAX + BLOCK + TAPS]
        filtered[start + GAUGE_MAX:start + GAUGE_MAX + BLOCK] = dot(toeplitz, window)

    masks = []
    for tile in range(n_tiles):
        lag = lag_ref[:, tile * 128:(tile + 1) * 128] - 1
        masks.append([lax.rem(lag // (2**b), 2) == 1 for b in range(4)])

    rows = BLOCK + GAUGE_MAX

    def difference(block):
        start = pl.multiple_of(block * BLOCK, BLOCK)
        for tile in range(n_tiles):
            cols = slice(tile * 128, (tile + 1) * 128)
            x = filtered[pl.ds(start, rows), cols]
            y = pltpu.roll(x, 1, 0)
            for b in (3, 2, 1, 0):
                y = jnp.where(jnp.broadcast_to(masks[tile][b], (rows, 128)), pltpu.roll(y, 2**b, 0), y)
            strain[pl.ds(start, BLOCK), cols] = (x - y)[GAUGE_MAX:].astype(BF16)

    for block in range(1, n_blocks):
        fir(block)

    @pl.loop(2, n_blocks)
    def _(block):
        difference(block)

    halo.wait()
    ext[pl.ds(0, HALO)] = jnp.where(tm == 0, jnp.zeros((HALO, n_cols), BF16), ext[pl.ds(0, HALO)])
    filtered[pl.ds(0, GAUGE_MAX)] = dot(toeplitz[:GAUGE_MAX, :HALO], ext[pl.ds(0, HALO)])
    fir(0)

    @pl.loop(0, 2)
    def _(block):
        difference(block)

    load_proj.wait()
    stk[0, 0:RANK] = dot(proj_ref[...], strain[...], TN)

    def remote(src, dst, send_sem, recv_sem, who):
        copy = pltpu.make_async_remote_copy(
            src_ref=src, dst_ref=dst, send_sem=send_sem, recv_sem=recv_sem, device_id=who, device_id_type=MESH)
        copy.start()
        return copy

    def send_diag(level):
        return remote(diag.at[level, 0], diag.at[level, 1], dg_sem.at[0, level], dg_sem.at[1, level],
                      {"tm": partners[level]})

    def scatter(j, value):
        part[j] = value.reshape(n_chan, slice_rows, RANK)
        scat[j, me] = part[j, me]
        copies = []
        for o in offsets:
            peer = lax.rem(me + o, n_chan)
            copies.append(remote(part.at[j, peer], scat.at[j, me], rs_send.at[j, o], rs_recv.at[j, o], {"chan": peer}))
        return copies

    def gather(j, copies):
        for copy in copies:
            copy.wait()
        gath[j, me] = jnp.sum(scat[j], axis=0)
        copies = []
        for o in offsets:
            peer = lax.rem(me + o, n_chan)
            copies.append(remote(gath.at[j, me], gath.at[j, me], ag_send.at[j, o], ag_recv.at[j, o], {"chan": peer}))
        return copies

    def finish(j, copies):
        for copy in copies:
            copy.wait()
        return gath[j].reshape(RANK, RANK)

    eye = (lax.broadcasted_iota(jnp.int32, (2 * RANK, 2 * RANK), 0)
           == lax.broadcasted_iota(jnp.int32, (2 * RANK, 2 * RANK), 1)).astype(F32)

    def split_rows(level, low, count):
        high, rest = split(stk[level, low:low + count])
        stk_hi[low:low + count] = high
        stk_lo[low:low + count] = rest
        return high, rest

    for level in range(levels):
        count = min(2**level, most)
        r = RANK // count
        h = r // 2
        last = level == levels - 1
        place = lax.rem(tm, count)
        mine_rows = pl.ds(pl.multiple_of(place * r, 8), r)
        got_rows = pl.ds(pl.multiple_of(RANK + place * r, 8), r)
        moving = remote(stk.at[level, mine_rows], stk.at[level, got_rows], ex_sem.at[0, level], ex_sem.at[1, level],
                        {"tm": partners[level]})
        own = split_rows(level, 0, RANK)
        if level == 0:
            diag_moving = scatter(0, dot3(own, own, NT))
            load_comp.wait()
            comp = comp_ref[...].T
            comp_t[0] = comp
            comp_t[1, :, 0:RANK] = comp[:, RANK:]
            comp_t[1, :, RANK:] = comp[:, :RANK]
            diag_moving = gather(0, diag_moving)
            moving.wait()
            cross_moving = scatter(1, dot3(split_rows(0, RANK, RANK), own, NT))
            diag[0, 0] = finish(0, diag_moving)
            diag_copy = send_diag(0)
            cross_moving = gather(1, cross_moving)
            below = finish(1, cross_moving)
        else:
            mix = (mix_hi[...], mix_lo[...])
            diag[level, 0] = dot3(split(dot3(mix, split(gram[...]))), mix, NT)
            diag_copy = send_diag(level)
            moving.wait()
            crossp[level, 0:r] = dot3(split(stk[level, got_rows]), own, NT)
            half = pl.ds(pl.multiple_of(core * h, 8), h)
            away = pl.ds(pl.multiple_of((1 - core) * h, 8), h)
            pre_copy = remote(crossp.at[level, away], pre.at[level, pl.ds(0, h)], pre_sem.at[0, level], pre_sem.at[1, level],
                              {"chan": other_core})
            forwards = []
            if not last:
                for i in range(1, count):
                    forwards.append(remote(stk.at[level, got_rows], stk.at[level, got_rows],
                                           f_send.at[level, i], f_recv.at[level, i], {"tm": member(count, i)}))
            pre_copy.wait()
            slot = zbuf.at[level, z_me, pl.ds(0, h)]
            slot[...] = crossp[level, half] + pre[level, 0:h]
            copies = []
            for o in z_offsets:
                peer = lax.rem(me + 2 * o, n_chan)
                copies.append(remote(slot, slot, z_send.at[level, o], z_recv.at[level, o], {"chan": peer}))
            for copy in copies:
                copy.wait()
            chunk = cross.at[level, pl.ds(pl.multiple_of(place * r + core * h, 8), h)]
            chunk[...] = jnp.sum(zbuf[level, :, 0:h], axis=0)
            copies = []
            for i in range(count - 1, -1, -1):
                for d in range(2):
                    if i + d > 0:
                        who = {"tm": member(count, i), "chan": me if d == 0 else other_core}
                        copies.append(remote(chunk, chunk, g_send.at[level, 2 * i + d], g_recv.at[level, 2 * i + d], who))
            for copy in forwards:
                copy.wait()
            if not last:
                split_rows(level, RANK, RANK)
            for copy in copies:
                copy.wait()
            below = cross[level]

        gram[RANK:, 0:RANK] = below
        gram[0:RANK, RANK:] = below.T
        gram[0:RANK, 0:RANK] = diag[level, 0]
        diag_copy.wait()
        gram[RANK:, RANK:] = diag[level, 1]

        value = gram[...]
        mean = jnp.sum(value * eye, keepdims=True) / (2 * RANK)
        shifted = value - mean * eye
        z = shifted / jnp.sqrt(jnp.sum(shifted * shifted, keepdims=True) + 1e-06)
        for step in range(K_ITERS):
            parts = split(z)
            z = 1.5 * z - 0.5 * dot3(parts, split(dot3(parts, parts)))

        upper = lax.rem(tm // 2**level, 2)
        if not last:
            mine = comp_t[upper]
            mix = split(0.5 * (mine + dot3(split(mine), split(z))))
            mix_hi[...], mix_lo[...] = mix
            stk[level + 1, 0:RANK] = dot3(mix, (stk_hi[...], stk_lo[...]))
        else:
            share = RANK // n_tm
            group = max(8, share)
            wanted = [comp_t[upper, pl.ds(pl.multiple_of(who * share // group * group, 8), group)]
                      for who in (tm, partners[level])]
            wanted = jnp.concatenate(wanted, 0)
            high, rest = split(z[:, 0:RANK])
            mix = split(0.5 * (wanted[:, 0:RANK] + dot3(split(wanted), (high, rest))))
            result = dot3(mix, own)

            def pick(block, who):
                spot = lax.rem(who, group // share)
                chosen = block[0:share]
                for i in range(1, group // share):
                    chosen = jnp.where(spot == i, block[i * share:(i + 1) * share], chosen)
                return chosen

            give[...] = pick(result[group:], partners[level])
            final = remote(give, take, last_sem.at[0], last_sem.at[1], {"tm": partners[level]})
            kept = pick(result[:group], tm)
            final.wait()
            out_ref[...] = kept + take[...]


def on_device(n_tm, n_chan, record, fir_taps, gauge_lag, projector, compress):
    n_rows, n_cols = record.shape
    levels = n_tm.bit_length() - 1
    base = lax.pad(lax.rev(fir_taps.astype(F32), (0,)), jnp.float32(0), ((1, 255 - TAPS, 0),)).reshape(1, 256)
    lag = gauge_lag.reshape(1, n_cols)
    slice_rows = RANK // n_chan
    most = min(MOST, n_tm)
    dma = pltpu.SemaphoreType.DMA
    vmem = pl.BlockSpec(memory_space=pltpu.VMEM)
    hbm = pl.BlockSpec(memory_space=pltpu.HBM)
    return pl.pallas_call(
        functools.partial(kernel, n_tm, n_chan, levels),
        out_shape=jax.ShapeDtypeStruct((RANK // n_tm, n_cols), F32),
        in_specs=[hbm, vmem, vmem, hbm, hbm],
        out_specs=vmem,
        scratch_shapes=[
            pltpu.VMEM((HALO + n_rows, n_cols), BF16),
            pltpu.VMEM((GAUGE_MAX + n_rows, n_cols), F32),
            pltpu.VMEM((n_rows, n_cols), BF16),
            pltpu.VMEM((n_rows, RANK), BF16),
            pltpu.VMEM((2 * RANK, RANK), F32),
            pltpu.VMEM((levels, 2 * RANK, n_cols), F32),
            pltpu.VMEM((2 * RANK, n_cols), BF16),
            pltpu.VMEM((2 * RANK, n_cols), BF16),
            pltpu.VMEM((2 * RANK, 2 * RANK), F32),
            pltpu.VMEM((levels, 2, RANK, RANK), F32),
            pltpu.VMEM((2, RANK, 2 * RANK), F32),
            pltpu.VMEM((2, n_chan, slice_rows, RANK), F32),
            pltpu.VMEM((2, n_chan, slice_rows, RANK), F32),
            pltpu.VMEM((2, n_chan, slice_rows, RANK), F32),
            pltpu.VMEM((levels, RANK // 2, RANK), F32),
            pltpu.VMEM((levels, RANK // 4, RANK), F32),
            pltpu.VMEM((levels, n_chan // 2, RANK // 4, RANK), F32),
            pltpu.VMEM((levels, RANK, RANK), F32),
            pltpu.VMEM((RANK // n_tm, n_cols), F32),
            pltpu.VMEM((RANK // n_tm, n_cols), F32),
            pltpu.VMEM((RANK, 2 * RANK), BF16),
            pltpu.VMEM((RANK, 2 * RANK), BF16),
            dma((3,)),
            dma((2,)),
            dma((2, levels)),
            dma((2, levels)),
            dma((2, n_chan)),
            dma((2, n_chan)),
            dma((2, n_chan)),
            dma((2, n_chan)),
            dma((2, levels)),
            dma((levels, n_chan // 2)),
            dma((levels, n_chan // 2)),
            dma((levels, 2 * most)),
            dma((levels, 2 * most)),
            dma((levels, most)),
            dma((levels, most)),
            dma((2,)),
        ],
        compiler_params=pltpu.CompilerParams(collective_id=0, has_side_effects=True, vmem_limit_bytes=40 * 2**20),
    )(record, base, lag, projector, compress)


def solution(mesh):
    return jax.shard_map(
        functools.partial(on_device, mesh.shape["tm"], mesh.shape["chan"]),
        mesh=mesh,
        in_specs=(P("tm", "chan"), P(), P("chan"), P("tm", None), P()),
        out_specs=P("tm", "chan"),
        check_vma=False,
    )
```

```python
import functools

import jax
import jax.numpy as jnp
from jax import lax
from jax.experimental import pallas as pl
from jax.experimental.pallas import tpu as pltpu
from jax.sharding import PartitionSpec as P

TAPS = 64
GAUGE_MAX = 16
K_ITERS = 8
HALO = 80
RANK = 128
BLOCK = 128
MOST = 8
MESH = pl.DeviceIdType.MESH
F32 = jnp.float32
BF16 = jnp.bfloat16


def split(value):
    high = value.astype(BF16)
    return high, (value - high.astype(F32)).astype(BF16)


def dot(first, second, contract=((1,), (0,))):
    return lax.dot_general(first, second, (contract, ((), ())), preferred_element_type=F32)


def dot3(first, second, contract=((1,), (0,))):
    fh, fl = first
    sh, sl = second
    return dot(fh, sh, contract) + (dot(fh, sl, contract) + dot(fl, sh, contract))


NT = ((1,), (1,))
TN = ((0,), (0,))


def kernel(n_tm, n_chan, levels, record, taps_hbm, lag_hbm, proj_hbm, comp_hbm, out_ref,
           ext, filtered, strain, proj_ref, comp_ref, taps_ref, lag_ref, stk, stk_hi, stk_lo, gram, diag, comp_t, part, scat, gath,
           crossp, pre, zbuf, cross, ahead, mix_hi, mix_lo,
           local_sem, halo_sem, ex_sem, dg_sem, rs_send, rs_recv, ag_send, ag_recv,
           pre_sem, z_send, z_recv, g_send, g_recv, f_send, f_recv):
    tm = lax.axis_index("tm")
    me = lax.axis_index("chan")
    n_rows, n_cols = record.shape
    slice_rows = RANK // n_chan
    n_blocks = n_rows // BLOCK
    n_tiles = n_cols // 128
    n_z = n_chan // 2
    core = lax.rem(me, 2)
    z_me = me // 2
    other_core = me + 1 - 2 * core

    load = pltpu.make_async_copy(record, ext.at[pl.ds(HALO, n_rows)], local_sem.at[0])
    load_proj = pltpu.make_async_copy(proj_hbm, proj_ref, local_sem.at[1])
    load_comp = pltpu.make_async_copy(comp_hbm, comp_ref, local_sem.at[2])
    load_taps = pltpu.make_async_copy(taps_hbm, taps_ref, local_sem.at[3])
    load_lag = pltpu.make_async_copy(lag_hbm, lag_ref, local_sem.at[4])
    load_taps.start()
    load_lag.start()
    load.start()
    load_proj.start()
    load_comp.start()

    nxt = lax.rem(tm + 1, n_tm)
    prv = lax.rem(tm + n_tm - 1, n_tm)
    partners = []
    for level in range(levels):
        bit = 2**level
        partners.append(tm + bit * (1 - 2 * lax.rem(tm // bit, 2)))
    offsets = sorted(range(1, n_chan), key=lambda o: -min(o, n_chan - o))
    z_offsets = sorted(range(1, n_z), key=lambda o: -min(o, n_z - o))
    most = min(MOST, n_tm)

    def member(count, i):
        return tm // count * count + lax.rem(tm + i, count)

    barrier = pltpu.get_barrier_semaphore()
    greeted = [{"tm": nxt}, {"tm": prv}]
    greeted += [{"tm": partners[level]} for level in range(levels) if 2**level >= most]
    greeted += [{"chan": lax.rem(me + o, n_chan)} for o in offsets]
    greeted += [{"tm": member(most, i), "chan": c} for i in range(1, most) for c in (me, other_core)]
    for who in greeted:
        pl.semaphore_signal(barrier, inc=1, device_id=who, device_id_type=MESH)

    load_taps.wait()
    load_lag.wait()
    taps = jnp.concatenate([taps_ref[...].astype(F32).reshape(1, TAPS), jnp.zeros((1, 256 - TAPS), F32)], 1)
    banded = pltpu.roll(jnp.broadcast_to(taps, (BLOCK + TAPS, 256)), 256 - TAPS, 1, stride=1, stride_axis=0)
    toeplitz = banded[:, 0:BLOCK].T.astype(BF16)
    load.wait()

    def fir(block):
        start = block * BLOCK
        window = ext[start + GAUGE_MAX:start + GAUGE_MAX + BLOCK + TAPS]
        filtered[start + GAUGE_MAX:start + GAUGE_MAX + BLOCK] = dot(toeplitz, window)

    masks = []
    for tile in range(n_tiles):
        lag = lag_ref[tile * 128:(tile + 1) * 128].reshape(1, 128) - 1
        masks.append([lax.rem(lag // (2**b), 2) == 1 for b in range(4)])

    rows = BLOCK + GAUGE_MAX

    def difference(block):
        start = pl.multiple_of(block * BLOCK, BLOCK)
        for tile in range(n_tiles):
            cols = slice(tile * 128, (tile + 1) * 128)
            x = filtered[pl.ds(start, rows), cols]
            y = pltpu.roll(x, 1, 0)
            for b in (3, 2, 1, 0):
                y = jnp.where(jnp.broadcast_to(masks[tile][b], (rows, 128)), pltpu.roll(y, 2**b, 0), y)
            strain[pl.ds(start, BLOCK), cols] = (x - y)[GAUGE_MAX:].astype(BF16)

    for block in range(1, n_blocks):
        fir(block)

    @pl.loop(2, n_blocks)
    def _(block):
        difference(block)

    pl.semaphore_wait(barrier, len(greeted))
    halo = pltpu.make_async_remote_copy(
        src_ref=record.at[pl.ds(n_rows - HALO, HALO)], dst_ref=ext.at[pl.ds(0, HALO)],
        send_sem=halo_sem.at[0], recv_sem=halo_sem.at[1], device_id={"tm": nxt}, device_id_type=MESH)
    halo.start()
    load_proj.wait()
    late = 2 * BLOCK
    stk[0, 0:RANK] = dot(proj_ref[late:], strain[late:], TN)
    load_comp.wait()
    comp = comp_ref[...].T
    comp_t[0] = comp
    comp_t[1, :, 0:RANK] = comp[:, RANK:]
    comp_t[1, :, RANK:] = comp[:, :RANK]
    halo.wait()
    ext[pl.ds(0, HALO)] = jnp.where(tm == 0, jnp.zeros((HALO, n_cols), BF16), ext[pl.ds(0, HALO)])
    filtered[pl.ds(0, GAUGE_MAX)] = dot(toeplitz[:GAUGE_MAX, :HALO], ext[pl.ds(0, HALO)])
    fir(0)

    @pl.loop(0, 2)
    def _(block):
        difference(block)

    stk[0, 0:RANK] += dot(proj_ref[0:late], strain[0:late], TN)

    def remote(src, dst, send_sem, recv_sem, who):
        copy = pltpu.make_async_remote_copy(
            src_ref=src, dst_ref=dst, send_sem=send_sem, recv_sem=recv_sem, device_id=who, device_id_type=MESH)
        copy.start()
        return copy

    def send_diag(level):
        return remote(diag.at[level, 0], diag.at[level, 1], dg_sem.at[0, level], dg_sem.at[1, level],
                      {"tm": partners[level]})

    def scatter(j, value):
        part[j] = value.reshape(n_chan, slice_rows, RANK)
        scat[j, me] = part[j, me]
        copies = []
        for o in offsets:
            peer = lax.rem(me + o, n_chan)
            copies.append(remote(part.at[j, peer], scat.at[j, me], rs_send.at[j, o], rs_recv.at[j, o], {"chan": peer}))
        return copies

    def gather(j, copies):
        for copy in copies:
            copy.wait()
        gath[j, me] = jnp.sum(scat[j], axis=0)
        copies = []
        for o in offsets:
            peer = lax.rem(me + o, n_chan)
            copies.append(remote(gath.at[j, me], gath.at[j, me], ag_send.at[j, o], ag_recv.at[j, o], {"chan": peer}))
        return copies

    def finish(j, copies):
        for copy in copies:
            copy.wait()
        return gath[j].reshape(RANK, RANK)

    eye = (lax.broadcasted_iota(jnp.int32, (2 * RANK, 2 * RANK), 0)
           == lax.broadcasted_iota(jnp.int32, (2 * RANK, 2 * RANK), 1)).astype(F32)

    def split_rows(level, low, count):
        high, rest = split(stk[level, low:low + count])
        stk_hi[low:low + count] = high
        stk_lo[low:low + count] = rest
        return high, rest

    for level in range(levels):
        count = min(2**level, most)
        r = RANK // count
        h = r // 2
        last = level == levels - 1
        place = lax.rem(tm, count)
        got_rows = pl.ds(pl.multiple_of(RANK + place * r, 8), r)
        if level == 0:
            moving = remote(stk.at[0, pl.ds(0, RANK)], stk.at[0, pl.ds(RANK, RANK)], ex_sem.at[0, 0], ex_sem.at[1, 0],
                            {"tm": partners[0]})
        own = split_rows(level, 0, RANK)
        if level == 0:
            diag_moving = scatter(0, dot3(own, own, NT))
            diag_moving = gather(0, diag_moving)
            moving.wait()
            cross_moving = scatter(1, dot3(split_rows(0, RANK, RANK), own, NT))
            diag[0, 0] = finish(0, diag_moving)
            diag_copy = send_diag(0)
            cross_moving = gather(1, cross_moving)
            below = finish(1, cross_moving)
        else:
            mix = (mix_hi[...], mix_lo[...])
            diag[level, 0] = dot3(split(dot3(mix, split(gram[...]))), mix, NT)
            diag_copy = send_diag(level)
            moving.wait()
            crossp[level, 0:r] = dot3(split(stk[level, got_rows]), own, NT)
            half = pl.ds(pl.multiple_of(core * h, 8), h)
            away = pl.ds(pl.multiple_of((1 - core) * h, 8), h)
            pre_copy = remote(crossp.at[level, away], pre.at[level, pl.ds(0, h)], pre_sem.at[0, level], pre_sem.at[1, level],
                              {"chan": other_core})
            forwards = []
            for i in range(1, count):
                forwards.append(remote(stk.at[level, got_rows], stk.at[level, got_rows],
                                       f_send.at[level, i], f_recv.at[level, i], {"tm": member(count, i)}))
            pre_copy.wait()
            slot = zbuf.at[level, z_me, pl.ds(0, h)]
            slot[...] = crossp[level, half] + pre[level, 0:h]
            copies = []
            for o in z_offsets:
                peer = lax.rem(me + 2 * o, n_chan)
                copies.append(remote(slot, slot, z_send.at[level, o], z_recv.at[level, o], {"chan": peer}))
            for copy in copies:
                copy.wait()
            chunk = cross.at[level, pl.ds(pl.multiple_of(place * r + core * h, 8), h)]
            chunk[...] = jnp.sum(zbuf[level, :, 0:h], axis=0)
            copies = []
            for i in range(count - 1, -1, -1):
                for d in range(2):
                    if i + d > 0:
                        who = {"tm": member(count, i), "chan": me if d == 0 else other_core}
                        copies.append(remote(chunk, chunk, g_send.at[level, 2 * i + d], g_recv.at[level, 2 * i + d], who))
            for copy in forwards:
                copy.wait()
            split_rows(level, RANK, RANK)
            for copy in copies:
                copy.wait()
            below = cross[level]

        gram[RANK:, 0:RANK] = below
        gram[0:RANK, RANK:] = below.T
        gram[0:RANK, 0:RANK] = diag[level, 0]
        diag_copy.wait()
        gram[RANK:, RANK:] = diag[level, 1]

        value = gram[...]
        mean = jnp.sum(value * eye, keepdims=True) / (2 * RANK)
        shifted = value - mean * eye
        z = shifted / jnp.sqrt(jnp.sum(shifted * shifted, keepdims=True) + 1e-06)
        for step in range(K_ITERS):
            parts = split(z)
            z = 1.5 * z - 0.5 * dot3(parts, split(dot3(parts, parts)))

        upper = lax.rem(tm // 2**level, 2)
        parts = split(z)
        both = (stk_hi[...], stk_lo[...])

        def mixed(rows):
            mine = comp_t[upper, rows]
            return split(0.5 * (mine + dot3(split(mine), parts)))

        if not last:
            after = min(2 * 2**level, most)
            size = RANK // after
            spot = lax.rem(tm, after) * size
            ahead[level + 1, 0:size] = dot3(mixed(pl.ds(pl.multiple_of(spot, 8), size)), both)
            moving = remote(ahead.at[level + 1, pl.ds(0, size)],
                            stk.at[level + 1, pl.ds(pl.multiple_of(RANK + spot, 8), size)],
                            ex_sem.at[0, level + 1], ex_sem.at[1, level + 1], {"tm": partners[level + 1]})
            mix = mixed(pl.ds(0, RANK))
            mix_hi[...], mix_lo[...] = mix
            stk[level + 1, 0:RANK] = dot3(mix, both)
        else:
            share = RANK // n_tm
            group = max(8, share)
            result = dot3(mixed(pl.ds(pl.multiple_of(tm * share // group * group, 8), group)), both)
            spot = lax.rem(tm, group // share)
            chosen = result[0:share]
            for i in range(1, group // share):
                chosen = jnp.where(spot == i, result[i * share:(i + 1) * share], chosen)
            out_ref[...] = chosen


def on_device(n_tm, n_chan, record, fir_taps, gauge_lag, projector, compress):
    n_rows, n_cols = record.shape
    levels = n_tm.bit_length() - 1
    slice_rows = RANK // n_chan
    most = min(MOST, n_tm)
    dma = pltpu.SemaphoreType.DMA
    vmem = pl.BlockSpec(memory_space=pltpu.VMEM)
    hbm = pl.BlockSpec(memory_space=pltpu.HBM)
    return pl.pallas_call(
        functools.partial(kernel, n_tm, n_chan, levels),
        out_shape=jax.ShapeDtypeStruct((RANK // n_tm, n_cols), F32),
        in_specs=[hbm] * 5,
        out_specs=vmem,
        scratch_shapes=[
            pltpu.VMEM((HALO + n_rows, n_cols), BF16),
            pltpu.VMEM((GAUGE_MAX + n_rows, n_cols), F32),
            pltpu.VMEM((n_rows, n_cols), BF16),
            pltpu.VMEM((n_rows, RANK), BF16),
            pltpu.VMEM((2 * RANK, RANK), F32),
            pltpu.VMEM((TAPS,), BF16),
            pltpu.VMEM((n_cols,), jnp.int32),
            pltpu.VMEM((levels, 2 * RANK, n_cols), F32),
            pltpu.VMEM((2 * RANK, n_cols), BF16),
            pltpu.VMEM((2 * RANK, n_cols), BF16),
            pltpu.VMEM((2 * RANK, 2 * RANK), F32),
            pltpu.VMEM((levels, 2, RANK, RANK), F32),
            pltpu.VMEM((2, RANK, 2 * RANK), F32),
            pltpu.VMEM((2, n_chan, slice_rows, RANK), F32),
            pltpu.VMEM((2, n_chan, slice_rows, RANK), F32),
            pltpu.VMEM((2, n_chan, slice_rows, RANK), F32),
            pltpu.VMEM((levels, RANK // 2, RANK), F32),
            pltpu.VMEM((levels, RANK // 4, RANK), F32),
            pltpu.VMEM((levels, n_chan // 2, RANK // 4, RANK), F32),
            pltpu.VMEM((levels, RANK, RANK), F32),
            pltpu.VMEM((levels, RANK // 2, n_cols), F32),
            pltpu.VMEM((RANK, 2 * RANK), BF16),
            pltpu.VMEM((RANK, 2 * RANK), BF16),
            dma((5,)),
            dma((2,)),
            dma((2, levels)),
            dma((2, levels)),
            dma((2, n_chan)),
            dma((2, n_chan)),
            dma((2, n_chan)),
            dma((2, n_chan)),
            dma((2, levels)),
            dma((levels, n_chan // 2)),
            dma((levels, n_chan // 2)),
            dma((levels, 2 * most)),
            dma((levels, 2 * most)),
            dma((levels, most)),
            dma((levels, most)),
        ],
        compiler_params=pltpu.CompilerParams(collective_id=0, has_side_effects=True, vmem_limit_bytes=67_000_000),
    )(record, fir_taps, gauge_lag, projector, compress)


def solution(mesh):
    return jax.shard_map(
        functools.partial(on_device, mesh.shape["tm"], mesh.shape["chan"]),
        mesh=mesh,
        in_specs=(P("tm", "chan"), P(), P("chan"), P("tm", None), P()),
        out_specs=P("tm", "chan"),
        check_vma=False,
    )
```

```python
import functools

import jax
import jax.numpy as jnp
from jax import lax
from jax.experimental import pallas as pl
from jax.experimental.pallas import tpu as pltpu
from jax.sharding import PartitionSpec as P

TAPS = 64
GAUGE_MAX = 16
K_ITERS = 8
HALO = 80
RANK = 128
BLOCK = 128
MOST = 8
COARSE = 5
MESH = pl.DeviceIdType.MESH
F32 = jnp.float32
BF16 = jnp.bfloat16


def split(value):
    high = value.astype(BF16)
    return high, (value - high.astype(F32)).astype(BF16)


def dot(first, second, contract=((1,), (0,))):
    return lax.dot_general(first, second, (contract, ((), ())), preferred_element_type=F32)


def dot3(first, second, contract=((1,), (0,))):
    fh, fl = first
    sh, sl = second
    return dot(fh, sh, contract) + (dot(fh, sl, contract) + dot(fl, sh, contract))


NT = ((1,), (1,))
TN = ((0,), (0,))


def kernel(n_tm, n_chan, levels, record, taps_hbm, lag_hbm, proj_hbm, comp_hbm, out_ref,
           ext, filtered, strain, proj_ref, comp_ref, taps_ref, lag_ref, stk, stk_hi, stk_lo, gram, diag, comp_t, part, scat, gath,
           crossp, pre, zbuf, wide, cross, ahead, mix_hi, mix_lo,
           local_sem, halo_sem, ex_sem, dg_sem, rs_send, rs_recv, ag_send, ag_recv,
           pre_sem, z_send, z_recv, g_send, g_recv, f_send, f_recv, w_send, w_recv):
    tm = lax.axis_index("tm")
    me = lax.axis_index("chan")
    n_rows, n_cols = record.shape
    slice_rows = RANK // n_chan
    n_blocks = n_rows // BLOCK
    n_tiles = n_cols // 128
    n_z = n_chan // 2
    core = lax.rem(me, 2)
    z_me = me // 2
    other_core = me + 1 - 2 * core

    load = pltpu.make_async_copy(record, ext.at[pl.ds(HALO, n_rows)], local_sem.at[0])
    load_proj = pltpu.make_async_copy(proj_hbm, proj_ref, local_sem.at[1])
    load_comp = pltpu.make_async_copy(comp_hbm, comp_ref, local_sem.at[2])
    load_taps = pltpu.make_async_copy(taps_hbm, taps_ref, local_sem.at[3])
    load_lag = pltpu.make_async_copy(lag_hbm, lag_ref, local_sem.at[4])
    load_taps.start()
    load_lag.start()
    load.start()
    load_proj.start()
    load_comp.start()

    nxt = lax.rem(tm + 1, n_tm)
    prv = lax.rem(tm + n_tm - 1, n_tm)
    partners = []
    for level in range(levels):
        bit = 2**level
        partners.append(tm + bit * (1 - 2 * lax.rem(tm // bit, 2)))
    offsets = sorted(range(1, n_chan), key=lambda o: -min(o, n_chan - o))
    z_offsets = sorted(range(1, n_z), key=lambda o: -min(o, n_z - o))
    most = min(MOST, n_tm)

    def member(count, i):
        return tm // count * count + lax.rem(tm + i, count)

    barrier = pltpu.get_barrier_semaphore()
    greeted = [{"tm": nxt}, {"tm": prv}]
    greeted += [{"tm": partners[level]} for level in range(levels) if 2**level >= most]
    greeted += [{"chan": lax.rem(me + o, n_chan)} for o in offsets]
    greeted += [{"tm": member(most, i), "chan": c} for i in range(1, most) for c in (me, other_core)]
    for who in greeted:
        pl.semaphore_signal(barrier, inc=1, device_id=who, device_id_type=MESH)

    load_taps.wait()
    load_lag.wait()
    taps = jnp.concatenate([taps_ref[...].astype(F32).reshape(1, TAPS), jnp.zeros((1, 256 - TAPS), F32)], 1)
    banded = pltpu.roll(jnp.broadcast_to(taps, (BLOCK + TAPS, 256)), 256 - TAPS, 1, stride=1, stride_axis=0)
    toeplitz = banded[:, 0:BLOCK].T.astype(BF16)
    load.wait()

    def fir(block):
        start = block * BLOCK
        window = ext[start + GAUGE_MAX:start + GAUGE_MAX + BLOCK + TAPS]
        filtered[start + GAUGE_MAX:start + GAUGE_MAX + BLOCK] = dot(toeplitz, window)

    masks = []
    for tile in range(n_tiles):
        lag = lag_ref[tile * 128:(tile + 1) * 128].reshape(1, 128) - 1
        masks.append([lax.rem(lag // (2**b), 2) == 1 for b in range(4)])

    rows = BLOCK + GAUGE_MAX

    def difference(block):
        start = pl.multiple_of(block * BLOCK, BLOCK)
        for tile in range(n_tiles):
            cols = slice(tile * 128, (tile + 1) * 128)
            x = filtered[pl.ds(start, rows), cols]
            y = pltpu.roll(x, 1, 0)
            for b in (3, 2, 1, 0):
                y = jnp.where(jnp.broadcast_to(masks[tile][b], (rows, 128)), pltpu.roll(y, 2**b, 0), y)
            strain[pl.ds(start, BLOCK), cols] = (x - y)[GAUGE_MAX:].astype(BF16)

    for block in range(1, n_blocks):
        fir(block)

    @pl.loop(2, n_blocks)
    def _(block):
        difference(block)

    pl.semaphore_wait(barrier, len(greeted))
    halo = pltpu.make_async_remote_copy(
        src_ref=record.at[pl.ds(n_rows - HALO, HALO)], dst_ref=ext.at[pl.ds(0, HALO)],
        send_sem=halo_sem.at[0], recv_sem=halo_sem.at[1], device_id={"tm": nxt}, device_id_type=MESH)
    halo.start()
    load_proj.wait()
    late = 2 * BLOCK
    stk[0, 0:RANK] = dot(proj_ref[late:], strain[late:], TN)
    load_comp.wait()
    comp = comp_ref[...].T
    comp_t[0] = comp
    comp_t[1, :, 0:RANK] = comp[:, RANK:]
    comp_t[1, :, RANK:] = comp[:, :RANK]
    halo.wait()
    ext[pl.ds(0, HALO)] = jnp.where(tm == 0, jnp.zeros((HALO, n_cols), BF16), ext[pl.ds(0, HALO)])
    filtered[pl.ds(0, GAUGE_MAX)] = dot(toeplitz[:GAUGE_MAX, :HALO], ext[pl.ds(0, HALO)])
    fir(0)

    @pl.loop(0, 2)
    def _(block):
        difference(block)

    stk[0, 0:RANK] += dot(proj_ref[0:late], strain[0:late], TN)

    def remote(src, dst, send_sem, recv_sem, who):
        copy = pltpu.make_async_remote_copy(
            src_ref=src, dst_ref=dst, send_sem=send_sem, recv_sem=recv_sem, device_id=who, device_id_type=MESH)
        copy.start()
        return copy

    def send_diag(level):
        return remote(diag.at[level, 0], diag.at[level, 1], dg_sem.at[0, level], dg_sem.at[1, level],
                      {"tm": partners[level]})

    def scatter(j, value):
        part[j] = value.reshape(n_chan, slice_rows, RANK)
        scat[j, me] = part[j, me]
        copies = []
        for o in offsets:
            peer = lax.rem(me + o, n_chan)
            copies.append(remote(part.at[j, peer], scat.at[j, me], rs_send.at[j, o], rs_recv.at[j, o], {"chan": peer}))
        return copies

    def gather(j, copies):
        for copy in copies:
            copy.wait()
        gath[j, me] = jnp.sum(scat[j], axis=0)
        copies = []
        for o in offsets:
            peer = lax.rem(me + o, n_chan)
            copies.append(remote(gath.at[j, me], gath.at[j, me], ag_send.at[j, o], ag_recv.at[j, o], {"chan": peer}))
        return copies

    def finish(j, copies):
        for copy in copies:
            copy.wait()
        return gath[j].reshape(RANK, RANK)

    eye = (lax.broadcasted_iota(jnp.int32, (2 * RANK, 2 * RANK), 0)
           == lax.broadcasted_iota(jnp.int32, (2 * RANK, 2 * RANK), 1)).astype(F32)

    def split_rows(level, low, count):
        high, rest = split(stk[level, low:low + count])
        stk_hi[low:low + count] = high
        stk_lo[low:low + count] = rest
        return high, rest

    for level in range(levels):
        count = min(2**level, most)
        r = RANK // count
        h = r // 2
        last = level == levels - 1
        place = lax.rem(tm, count)
        got_rows = pl.ds(pl.multiple_of(RANK + place * r, 8), r)
        if level == 0:
            moving = remote(stk.at[0, pl.ds(0, RANK)], stk.at[0, pl.ds(RANK, RANK)], ex_sem.at[0, 0], ex_sem.at[1, 0],
                            {"tm": partners[0]})
        own = split_rows(level, 0, RANK)
        if level == 0:
            diag_moving = scatter(0, dot3(own, own, NT))
            diag_moving = gather(0, diag_moving)
            moving.wait()
            cross_moving = scatter(1, dot3(split_rows(0, RANK, RANK), own, NT))
            diag[0, 0] = finish(0, diag_moving)
            diag_copy = send_diag(0)
            cross_moving = gather(1, cross_moving)
            below = finish(1, cross_moving)
        else:
            mix = (mix_hi[...], mix_lo[...])
            diag[level, 0] = dot3(split(dot3(mix, split(gram[...]))), mix, NT)
            diag_copy = send_diag(level)
            moving.wait()
            crossp[level, 0:r] = dot3(split(stk[level, got_rows]), own, NT)
            half = pl.ds(pl.multiple_of(core * h, 8), h)
            away = pl.ds(pl.multiple_of((1 - core) * h, 8), h)
            direct = h == 8
            if direct:
                peers = []
                for o in offsets:
                    peer = lax.rem(me + o, n_chan)
                    rows_there = pl.ds(pl.multiple_of(lax.rem(peer, 2) * h, 8), h)
                    peers.append(remote(crossp.at[level, rows_there], wide.at[level, me],
                                        w_send.at[level, o], w_recv.at[level, o], {"chan": peer}))
                wide[level, me] = crossp[level, half]
            else:
                pre_copy = remote(crossp.at[level, away], pre.at[level, pl.ds(0, h)],
                                  pre_sem.at[0, level], pre_sem.at[1, level], {"chan": other_core})
            forwards = []
            for i in range(1, count):
                forwards.append(remote(stk.at[level, got_rows], stk.at[level, got_rows],
                                       f_send.at[level, i], f_recv.at[level, i], {"tm": member(count, i)}))
            if direct:
                for copy in peers:
                    copy.wait()
                total = jnp.sum(wide[level], axis=0)
            else:
                pre_copy.wait()
                slot = zbuf.at[level, z_me, pl.ds(0, h)]
                slot[...] = crossp[level, half] + pre[level, 0:h]
                copies = []
                for o in z_offsets:
                    peer = lax.rem(me + 2 * o, n_chan)
                    copies.append(remote(slot, slot, z_send.at[level, o], z_recv.at[level, o], {"chan": peer}))
                for copy in copies:
                    copy.wait()
                total = jnp.sum(zbuf[level, :, 0:h], axis=0)
            chunk = cross.at[level, pl.ds(pl.multiple_of(place * r + core * h, 8), h)]
            chunk[...] = total
            copies = []
            for i in range(count - 1, -1, -1):
                for d in range(2):
                    if i + d > 0:
                        who = {"tm": member(count, i), "chan": me if d == 0 else other_core}
                        copies.append(remote(chunk, chunk, g_send.at[level, 2 * i + d], g_recv.at[level, 2 * i + d], who))
            for copy in forwards:
                copy.wait()
            split_rows(level, RANK, RANK)
            for copy in copies:
                copy.wait()
            below = cross[level]

        gram[RANK:, 0:RANK] = below
        gram[0:RANK, RANK:] = below.T
        gram[0:RANK, 0:RANK] = diag[level, 0]
        diag_copy.wait()
        gram[RANK:, RANK:] = diag[level, 1]

        value = gram[...]
        mean = jnp.sum(value * eye, keepdims=True) / (2 * RANK)
        shifted = value - mean * eye
        z = shifted / jnp.sqrt(jnp.sum(shifted * shifted, keepdims=True) + 1e-06)
        for step in range(K_ITERS):
            if step < COARSE:
                rounded = z.astype(BF16)
                z = 1.5 * z - 0.5 * dot(rounded, dot(rounded, rounded).astype(BF16))
                continue
            parts = split(z)
            z = 1.5 * z - 0.5 * dot3(parts, split(dot3(parts, parts)))

        upper = lax.rem(tm // 2**level, 2)
        parts = split(z)
        both = (stk_hi[...], stk_lo[...])

        def mixed(rows):
            mine = comp_t[upper, rows]
            return split(0.5 * (mine + dot3(split(mine), parts)))

        if not last:
            after = min(2 * 2**level, most)
            size = RANK // after
            spot = lax.rem(tm, after) * size
            ahead[level + 1, 0:size] = dot3(mixed(pl.ds(pl.multiple_of(spot, 8), size)), both)
            moving = remote(ahead.at[level + 1, pl.ds(0, size)],
                            stk.at[level + 1, pl.ds(pl.multiple_of(RANK + spot, 8), size)],
                            ex_sem.at[0, level + 1], ex_sem.at[1, level + 1], {"tm": partners[level + 1]})
            mix = mixed(pl.ds(0, RANK))
            mix_hi[...], mix_lo[...] = mix
            stk[level + 1, 0:RANK] = dot3(mix, both)
        else:
            share = RANK // n_tm
            group = max(8, share)
            result = dot3(mixed(pl.ds(pl.multiple_of(tm * share // group * group, 8), group)), both)
            spot = lax.rem(tm, group // share)
            chosen = result[0:share]
            for i in range(1, group // share):
                chosen = jnp.where(spot == i, result[i * share:(i + 1) * share], chosen)
            out_ref[...] = chosen


def on_device(n_tm, n_chan, record, fir_taps, gauge_lag, projector, compress):
    n_rows, n_cols = record.shape
    levels = n_tm.bit_length() - 1
    slice_rows = RANK // n_chan
    most = min(MOST, n_tm)
    dma = pltpu.SemaphoreType.DMA
    vmem = pl.BlockSpec(memory_space=pltpu.VMEM)
    hbm = pl.BlockSpec(memory_space=pltpu.HBM)
    return pl.pallas_call(
        functools.partial(kernel, n_tm, n_chan, levels),
        out_shape=jax.ShapeDtypeStruct((RANK // n_tm, n_cols), F32),
        in_specs=[hbm] * 5,
        out_specs=vmem,
        scratch_shapes=[
            pltpu.VMEM((HALO + n_rows, n_cols), BF16),
            pltpu.VMEM((GAUGE_MAX + n_rows, n_cols), F32),
            pltpu.VMEM((n_rows, n_cols), BF16),
            pltpu.VMEM((n_rows, RANK), BF16),
            pltpu.VMEM((2 * RANK, RANK), F32),
            pltpu.VMEM((TAPS,), BF16),
            pltpu.VMEM((n_cols,), jnp.int32),
            pltpu.VMEM((levels, 2 * RANK, n_cols), F32),
            pltpu.VMEM((2 * RANK, n_cols), BF16),
            pltpu.VMEM((2 * RANK, n_cols), BF16),
            pltpu.VMEM((2 * RANK, 2 * RANK), F32),
            pltpu.VMEM((levels, 2, RANK, RANK), F32),
            pltpu.VMEM((2, RANK, 2 * RANK), F32),
            pltpu.VMEM((2, n_chan, slice_rows, RANK), F32),
            pltpu.VMEM((2, n_chan, slice_rows, RANK), F32),
            pltpu.VMEM((2, n_chan, slice_rows, RANK), F32),
            pltpu.VMEM((levels, RANK // 2, RANK), F32),
            pltpu.VMEM((levels, RANK // 4, RANK), F32),
            pltpu.VMEM((levels, n_chan // 2, RANK // 4, RANK), F32),
            pltpu.VMEM((levels, n_chan, 8, RANK), F32),
            pltpu.VMEM((levels, RANK, RANK), F32),
            pltpu.VMEM((levels, RANK // 2, n_cols), F32),
            pltpu.VMEM((RANK, 2 * RANK), BF16),
            pltpu.VMEM((RANK, 2 * RANK), BF16),
            dma((5,)),
            dma((2,)),
            dma((2, levels)),
            dma((2, levels)),
            dma((2, n_chan)),
            dma((2, n_chan)),
            dma((2, n_chan)),
            dma((2, n_chan)),
            dma((2, levels)),
            dma((levels, n_chan // 2)),
            dma((levels, n_chan // 2)),
            dma((levels, 2 * most)),
            dma((levels, 2 * most)),
            dma((levels, most)),
            dma((levels, most)),
            dma((levels, n_chan)),
            dma((levels, n_chan)),
        ],
        compiler_params=pltpu.CompilerParams(collective_id=0, has_side_effects=True, vmem_limit_bytes=67_000_000),
    )(record, fir_taps, gauge_lag, projector, compress)


def solution(mesh):
    return jax.shard_map(
        functools.partial(on_device, mesh.shape["tm"], mesh.shape["chan"]),
        mesh=mesh,
        in_specs=(P("tm", "chan"), P(), P("chan"), P("tm", None), P()),
        out_specs=P("tm", "chan"),
        check_vma=False,
    )
```

```python
import functools

import jax
import jax.numpy as jnp
from jax import lax
from jax.experimental import pallas as pl
from jax.experimental.pallas import tpu as pltpu
from jax.sharding import PartitionSpec as P

TAPS = 64
GAUGE_MAX = 16
K_ITERS = 8
HALO = 80
RANK = 128
BLOCK = 128
MOST = 8
COARSE = 7
MESH = pl.DeviceIdType.MESH
F32 = jnp.float32
BF16 = jnp.bfloat16


def split(value):
    high = value.astype(BF16)
    return high, (value - high.astype(F32)).astype(BF16)


def dot(first, second, contract=((1,), (0,))):
    return lax.dot_general(first, second, (contract, ((), ())), preferred_element_type=F32)


def dot3(first, second, contract=((1,), (0,))):
    fh, fl = first
    sh, sl = second
    return dot(fh, sh, contract) + (dot(fh, sl, contract) + dot(fl, sh, contract))


NT = ((1,), (1,))
TN = ((0,), (0,))


def kernel(n_tm, n_chan, levels, record, taps_hbm, lag_hbm, proj_hbm, comp_hbm, out_ref,
           ext, filtered, strain, proj_ref, comp_ref, taps_ref, lag_ref, stk, stk_hi, stk_lo, gram, diag, comp_t, part, scat, gath,
           crossp, pre, zbuf, wide, cross, ahead_hi, ahead_lo, mix_hi, mix_lo,
           local_sem, halo_sem, ex_sem, dg_sem, rs_send, rs_recv, ag_send, ag_recv,
           pre_sem, z_send, z_recv, g_send, g_recv, f_send, f_recv, w_send, w_recv):
    tm = lax.axis_index("tm")
    me = lax.axis_index("chan")
    n_rows, n_cols = record.shape
    slice_rows = RANK // n_chan
    n_blocks = n_rows // BLOCK
    n_tiles = n_cols // 128
    n_z = n_chan // 2
    core = lax.rem(me, 2)
    z_me = me // 2
    other_core = me + 1 - 2 * core

    load = pltpu.make_async_copy(record, ext.at[pl.ds(HALO, n_rows)], local_sem.at[0])
    load_proj = pltpu.make_async_copy(proj_hbm, proj_ref, local_sem.at[1])
    load_comp = pltpu.make_async_copy(comp_hbm, comp_ref, local_sem.at[2])
    load_taps = pltpu.make_async_copy(taps_hbm, taps_ref, local_sem.at[3])
    load_lag = pltpu.make_async_copy(lag_hbm, lag_ref, local_sem.at[4])
    load_taps.start()
    load_lag.start()
    load.start()
    load_proj.start()
    load_comp.start()

    nxt = lax.rem(tm + 1, n_tm)
    prv = lax.rem(tm + n_tm - 1, n_tm)
    partners = []
    for level in range(levels):
        bit = 2**level
        partners.append(tm + bit * (1 - 2 * lax.rem(tm // bit, 2)))
    offsets = sorted(range(1, n_chan), key=lambda o: -min(o, n_chan - o))
    z_offsets = sorted(range(1, n_z), key=lambda o: -min(o, n_z - o))
    most = min(MOST, n_tm)

    def member(count, i):
        return tm // count * count + lax.rem(tm + i, count)

    barrier = pltpu.get_barrier_semaphore()
    greeted = [{"tm": nxt}, {"tm": prv}]
    greeted += [{"tm": partners[level]} for level in range(levels) if 2**level >= most]
    greeted += [{"chan": lax.rem(me + o, n_chan)} for o in offsets]
    greeted += [{"tm": member(most, i), "chan": c} for i in range(1, most) for c in (me, other_core)]
    for who in greeted:
        pl.semaphore_signal(barrier, inc=1, device_id=who, device_id_type=MESH)

    load_taps.wait()
    load_lag.wait()
    taps = jnp.concatenate([taps_ref[...].astype(F32).reshape(1, TAPS), jnp.zeros((1, 256 - TAPS), F32)], 1)
    banded = pltpu.roll(jnp.broadcast_to(taps, (BLOCK + TAPS, 256)), 256 - TAPS, 1, stride=1, stride_axis=0)
    toeplitz = banded[:, 0:BLOCK].T.astype(BF16)
    load.wait()

    def fir(block):
        start = block * BLOCK
        window = ext[start + GAUGE_MAX:start + GAUGE_MAX + BLOCK + TAPS]
        filtered[start + GAUGE_MAX:start + GAUGE_MAX + BLOCK] = dot(toeplitz, window)

    masks = []
    for tile in range(n_tiles):
        lag = lag_ref[tile * 128:(tile + 1) * 128].reshape(1, 128) - 1
        masks.append([lax.rem(lag // (2**b), 2) == 1 for b in range(4)])

    rows = BLOCK + GAUGE_MAX

    def difference(block):
        start = pl.multiple_of(block * BLOCK, BLOCK)
        for tile in range(n_tiles):
            cols = slice(tile * 128, (tile + 1) * 128)
            x = filtered[pl.ds(start, rows), cols]
            y = pltpu.roll(x, 1, 0)
            for b in (3, 2, 1, 0):
                y = jnp.where(jnp.broadcast_to(masks[tile][b], (rows, 128)), pltpu.roll(y, 2**b, 0), y)
            strain[pl.ds(start, BLOCK), cols] = (x - y)[GAUGE_MAX:].astype(BF16)

    for block in range(1, n_blocks):
        fir(block)

    @pl.loop(2, n_blocks)
    def _(block):
        difference(block)

    pl.semaphore_wait(barrier, len(greeted))
    halo = pltpu.make_async_remote_copy(
        src_ref=record.at[pl.ds(n_rows - HALO, HALO)], dst_ref=ext.at[pl.ds(0, HALO)],
        send_sem=halo_sem.at[0], recv_sem=halo_sem.at[1], device_id={"tm": nxt}, device_id_type=MESH)
    halo.start()
    load_proj.wait()
    late = 2 * BLOCK
    stk[0] = dot(proj_ref[late:], strain[late:], TN)
    load_comp.wait()
    comp = comp_ref[...].T
    comp_t[0] = comp
    comp_t[1, :, 0:RANK] = comp[:, RANK:]
    comp_t[1, :, RANK:] = comp[:, :RANK]
    halo.wait()
    ext[pl.ds(0, HALO)] = jnp.where(tm == 0, jnp.zeros((HALO, n_cols), BF16), ext[pl.ds(0, HALO)])
    filtered[pl.ds(0, GAUGE_MAX)] = dot(toeplitz[:GAUGE_MAX, :HALO], ext[pl.ds(0, HALO)])
    fir(0)

    @pl.loop(0, 2)
    def _(block):
        difference(block)

    stk[0] += dot(proj_ref[0:late], strain[0:late], TN)

    def remote(src, dst, send_sem, recv_sem, who):
        copy = pltpu.make_async_remote_copy(
            src_ref=src, dst_ref=dst, send_sem=send_sem, recv_sem=recv_sem, device_id=who, device_id_type=MESH)
        copy.start()
        return copy

    def send_diag(level):
        return remote(diag.at[level, 0], diag.at[level, 1], dg_sem.at[0, level], dg_sem.at[1, level],
                      {"tm": partners[level]})

    def scatter(j, value):
        part[j] = value.reshape(n_chan, slice_rows, RANK)
        scat[j, me] = part[j, me]
        copies = []
        for o in offsets:
            peer = lax.rem(me + o, n_chan)
            copies.append(remote(part.at[j, peer], scat.at[j, me], rs_send.at[j, o], rs_recv.at[j, o], {"chan": peer}))
        return copies

    def gather(j, copies):
        for copy in copies:
            copy.wait()
        gath[j, me] = jnp.sum(scat[j], axis=0)
        copies = []
        for o in offsets:
            peer = lax.rem(me + o, n_chan)
            copies.append(remote(gath.at[j, me], gath.at[j, me], ag_send.at[j, o], ag_recv.at[j, o], {"chan": peer}))
        return copies

    def finish(j, copies):
        for copy in copies:
            copy.wait()
        return gath[j].reshape(RANK, RANK)

    eye = (lax.broadcasted_iota(jnp.int32, (2 * RANK, 2 * RANK), 0)
           == lax.broadcasted_iota(jnp.int32, (2 * RANK, 2 * RANK), 1)).astype(F32)

    def split_rows(level):
        high, rest = split(stk[level])
        stk_hi[level, 0:RANK] = high
        stk_lo[level, 0:RANK] = rest
        return high, rest

    def send_rows(level, high, rest, where):
        who = {"tm": partners[level]}
        return (remote(high, stk_hi.at[level, where], ex_sem.at[0, level], ex_sem.at[1, level], who),
                remote(rest, stk_lo.at[level, where], ex_sem.at[2, level], ex_sem.at[3, level], who))

    def cross_rows(received, own):
        return dot(received, own[0], NT) + dot(received, own[1], NT)

    for level in range(levels):
        count = min(2**level, most)
        r = RANK // count
        h = r // 2
        last = level == levels - 1
        place = lax.rem(tm, count)
        got_rows = pl.ds(pl.multiple_of(RANK + place * r, 16), r)
        own = split_rows(level)
        if level == 0:
            upper_half = pl.ds(RANK, RANK)
            moving, moving_low = send_rows(0, stk_hi.at[0, pl.ds(0, RANK)], stk_lo.at[0, pl.ds(0, RANK)], upper_half)
        if level == 0:
            diag_moving = scatter(0, dot3(own, own, NT))
            diag_moving = gather(0, diag_moving)
            moving.wait()
            cross_moving = scatter(1, cross_rows(stk_hi[0, RANK:], own))
            moving_low.wait()
            diag[0, 0] = finish(0, diag_moving)
            diag_copy = send_diag(0)
            cross_moving = gather(1, cross_moving)
            below = finish(1, cross_moving)
        else:
            mix = (mix_hi[...], mix_lo[...])
            diag[level, 0] = dot3(split(dot3(mix, split(gram[...]))), mix, NT)
            diag_copy = send_diag(level)
            moving.wait()
            crossp[level, 0:r] = cross_rows(stk_hi[level, got_rows], own)
            half = pl.ds(pl.multiple_of(core * h, 8), h)
            away = pl.ds(pl.multiple_of((1 - core) * h, 8), h)
            direct = h == 8
            if direct:
                peers = []
                for o in offsets:
                    peer = lax.rem(me + o, n_chan)
                    rows_there = pl.ds(pl.multiple_of(lax.rem(peer, 2) * h, 8), h)
                    peers.append(remote(crossp.at[level, rows_there], wide.at[level, me],
                                        w_send.at[level, o], w_recv.at[level, o], {"chan": peer}))
                wide[level, me] = crossp[level, half]
            else:
                pre_copy = remote(crossp.at[level, away], pre.at[level, pl.ds(0, h)],
                                  pre_sem.at[0, level], pre_sem.at[1, level], {"chan": other_core})
            forwards = []
            moving_low.wait()
            for i in range(1, count):
                for k, side in enumerate((stk_hi, stk_lo)):
                    forwards.append(remote(side.at[level, got_rows], side.at[level, got_rows],
                                           f_send.at[level, 2 * i + k], f_recv.at[level, 2 * i + k],
                                           {"tm": member(count, i)}))
            if direct:
                for copy in peers:
                    copy.wait()
                total = jnp.sum(wide[level], axis=0)
            else:
                pre_copy.wait()
                slot = zbuf.at[level, z_me, pl.ds(0, h)]
                slot[...] = crossp[level, half] + pre[level, 0:h]
                copies = []
                for o in z_offsets:
                    peer = lax.rem(me + 2 * o, n_chan)
                    copies.append(remote(slot, slot, z_send.at[level, o], z_recv.at[level, o], {"chan": peer}))
                for copy in copies:
                    copy.wait()
                total = jnp.sum(zbuf[level, :, 0:h], axis=0)
            chunk = cross.at[level, pl.ds(pl.multiple_of(place * r + core * h, 8), h)]
            chunk[...] = total
            copies = []
            for i in range(count - 1, -1, -1):
                for d in range(2):
                    if i + d > 0:
                        who = {"tm": member(count, i), "chan": me if d == 0 else other_core}
                        copies.append(remote(chunk, chunk, g_send.at[level, 2 * i + d], g_recv.at[level, 2 * i + d], who))
            for copy in forwards:
                copy.wait()
            for copy in copies:
                copy.wait()
            below = cross[level]

        gram[RANK:, 0:RANK] = below
        gram[0:RANK, RANK:] = below.T
        gram[0:RANK, 0:RANK] = diag[level, 0]
        diag_copy.wait()
        gram[RANK:, RANK:] = diag[level, 1]

        value = gram[...]
        mean = jnp.sum(value * eye, keepdims=True) / (2 * RANK)
        shifted = value - mean * eye
        z = shifted / jnp.sqrt(jnp.sum(shifted * shifted, keepdims=True) + 1e-06)
        for step in range(K_ITERS):
            if step < COARSE:
                rounded = z.astype(BF16)
                z = 1.5 * z - 0.5 * dot(rounded, dot(rounded, rounded).astype(BF16))
                continue
            parts = split(z)
            z = 1.5 * z - 0.5 * dot3(parts, split(dot3(parts, parts)))

        upper = lax.rem(tm // 2**level, 2)
        parts = split(z)
        both = (stk_hi[level], stk_lo[level])

        def mixed(rows):
            mine = comp_t[upper, rows]
            return split(0.5 * (mine + dot3(split(mine), parts)))

        if not last:
            after = min(2 * 2**level, most)
            size = RANK // after
            spot = lax.rem(tm, after) * size
            early, early_low = split(dot3(mixed(pl.ds(pl.multiple_of(spot, 16), size)), both))
            ahead_hi[level + 1, 0:size] = early
            ahead_lo[level + 1, 0:size] = early_low
            moving, moving_low = send_rows(level + 1, ahead_hi.at[level + 1, pl.ds(0, size)],
                                           ahead_lo.at[level + 1, pl.ds(0, size)],
                                           pl.ds(pl.multiple_of(RANK + spot, 16), size))
            mix = mixed(pl.ds(0, RANK))
            mix_hi[...], mix_lo[...] = mix
            stk[level + 1] = dot3(mix, both)
        else:
            share = RANK // n_tm
            group = max(8, share)
            result = dot3(mixed(pl.ds(pl.multiple_of(tm * share // group * group, 8), group)), both)
            spot = lax.rem(tm, group // share)
            chosen = result[0:share]
            for i in range(1, group // share):
                chosen = jnp.where(spot == i, result[i * share:(i + 1) * share], chosen)
            out_ref[...] = chosen


def on_device(n_tm, n_chan, record, fir_taps, gauge_lag, projector, compress):
    n_rows, n_cols = record.shape
    levels = n_tm.bit_length() - 1
    slice_rows = RANK // n_chan
    most = min(MOST, n_tm)
    dma = pltpu.SemaphoreType.DMA
    vmem = pl.BlockSpec(memory_space=pltpu.VMEM)
    hbm = pl.BlockSpec(memory_space=pltpu.HBM)
    return pl.pallas_call(
        functools.partial(kernel, n_tm, n_chan, levels),
        out_shape=jax.ShapeDtypeStruct((RANK // n_tm, n_cols), F32),
        in_specs=[hbm] * 5,
        out_specs=vmem,
        scratch_shapes=[
            pltpu.VMEM((HALO + n_rows, n_cols), BF16),
            pltpu.VMEM((GAUGE_MAX + n_rows, n_cols), F32),
            pltpu.VMEM((n_rows, n_cols), BF16),
            pltpu.VMEM((n_rows, RANK), BF16),
            pltpu.VMEM((2 * RANK, RANK), F32),
            pltpu.VMEM((TAPS,), BF16),
            pltpu.VMEM((n_cols,), jnp.int32),
            pltpu.VMEM((levels, RANK, n_cols), F32),
            pltpu.VMEM((levels, 2 * RANK, n_cols), BF16),
            pltpu.VMEM((levels, 2 * RANK, n_cols), BF16),
            pltpu.VMEM((2 * RANK, 2 * RANK), F32),
            pltpu.VMEM((levels, 2, RANK, RANK), F32),
            pltpu.VMEM((2, RANK, 2 * RANK), F32),
            pltpu.VMEM((2, n_chan, slice_rows, RANK), F32),
            pltpu.VMEM((2, n_chan, slice_rows, RANK), F32),
            pltpu.VMEM((2, n_chan, slice_rows, RANK), F32),
            pltpu.VMEM((levels, RANK // 2, RANK), F32),
            pltpu.VMEM((levels, RANK // 4, RANK), F32),
            pltpu.VMEM((levels, n_chan // 2, RANK // 4, RANK), F32),
            pltpu.VMEM((levels, n_chan, 8, RANK), F32),
            pltpu.VMEM((levels, RANK, RANK), F32),
            pltpu.VMEM((levels, RANK // 2, n_cols), BF16),
            pltpu.VMEM((levels, RANK // 2, n_cols), BF16),
            pltpu.VMEM((RANK, 2 * RANK), BF16),
            pltpu.VMEM((RANK, 2 * RANK), BF16),
            dma((5,)),
            dma((2,)),
            dma((4, levels)),
            dma((2, levels)),
            dma((2, n_chan)),
            dma((2, n_chan)),
            dma((2, n_chan)),
            dma((2, n_chan)),
            dma((2, levels)),
            dma((levels, n_chan // 2)),
            dma((levels, n_chan // 2)),
            dma((levels, 2 * most)),
            dma((levels, 2 * most)),
            dma((levels, 2 * most)),
            dma((levels, 2 * most)),
            dma((levels, n_chan)),
            dma((levels, n_chan)),
        ],
        compiler_params=pltpu.CompilerParams(collective_id=0, has_side_effects=True, vmem_limit_bytes=67_000_000),
    )(record, fir_taps, gauge_lag, projector, compress)


def solution(mesh):
    return jax.shard_map(
        functools.partial(on_device, mesh.shape["tm"], mesh.shape["chan"]),
        mesh=mesh,
        in_specs=(P("tm", "chan"), P(), P("chan"), P("tm", None), P()),
        out_specs=P("tm", "chan"),
        check_vma=False,
    )
```

```python
import functools

import jax
import jax.numpy as jnp
from jax import lax
from jax.experimental import pallas as pl
from jax.experimental.pallas import tpu as pltpu
from jax.sharding import PartitionSpec as P

TAPS = 64
GAUGE_MAX = 16
K_ITERS = 8
HALO = 80
RANK = 128
BLOCK = 128
MOST = 8
COARSE = 7
MESH = pl.DeviceIdType.MESH
F32 = jnp.float32
BF16 = jnp.bfloat16


def split(value):
    high = value.astype(BF16)
    return high, (value - high.astype(F32)).astype(BF16)


def dot(first, second, contract=((1,), (0,))):
    return lax.dot_general(first, second, (contract, ((), ())), preferred_element_type=F32)


def dot3(first, second, contract=((1,), (0,))):
    fh, fl = first
    sh, sl = second
    return dot(fh, sh, contract) + (dot(fh, sl, contract) + dot(fl, sh, contract))


NT = ((1,), (1,))
TN = ((0,), (0,))


def kernel(n_tm, n_chan, levels, record, taps_hbm, lag_hbm, proj_hbm, comp_hbm, out_ref,
           ext, filtered, strain, proj_ref, comp_ref, taps_ref, lag_ref, stk, stk_hi, stk_lo, gram, diag, comp_t, part, scat, gath,
           crossp, crossp_b, pre, zbuf, wide, cross, cross_b, ahead_hi, ahead_lo, mix_hi, mix_lo,
           local_sem, halo_sem, ex_sem, dg_sem, rs_send, rs_recv, ag_send, ag_recv,
           pre_sem, z_send, z_recv, g_send, g_recv, f_send, f_recv, w_send, w_recv):
    tm = lax.axis_index("tm")
    me = lax.axis_index("chan")
    n_rows, n_cols = record.shape
    slice_rows = RANK // n_chan
    n_blocks = n_rows // BLOCK
    n_tiles = n_cols // 128
    n_z = n_chan // 2
    core = lax.rem(me, 2)
    z_me = me // 2
    other_core = me + 1 - 2 * core

    load = pltpu.make_async_copy(record, ext.at[pl.ds(HALO, n_rows)], local_sem.at[0])
    load_proj = pltpu.make_async_copy(proj_hbm, proj_ref, local_sem.at[1])
    load_comp = pltpu.make_async_copy(comp_hbm, comp_ref, local_sem.at[2])
    load_taps = pltpu.make_async_copy(taps_hbm, taps_ref, local_sem.at[3])
    load_lag = pltpu.make_async_copy(lag_hbm, lag_ref, local_sem.at[4])
    load_taps.start()
    load_lag.start()
    load.start()
    load_proj.start()
    load_comp.start()

    nxt = lax.rem(tm + 1, n_tm)
    prv = lax.rem(tm + n_tm - 1, n_tm)
    partners = []
    for level in range(levels):
        bit = 2**level
        partners.append(tm + bit * (1 - 2 * lax.rem(tm // bit, 2)))
    offsets = sorted(range(1, n_chan), key=lambda o: -min(o, n_chan - o))
    z_offsets = sorted(range(1, n_z), key=lambda o: -min(o, n_z - o))
    most = min(MOST, n_tm)

    def member(count, i):
        return tm // count * count + lax.rem(tm + i, count)

    barrier = pltpu.get_barrier_semaphore()
    greeted = [{"tm": nxt}, {"tm": prv}]
    greeted += [{"tm": partners[level]} for level in range(levels) if 2**level >= most]
    greeted += [{"chan": lax.rem(me + o, n_chan)} for o in offsets]
    greeted += [{"tm": member(most, i), "chan": c} for i in range(1, most) for c in (me, other_core)]
    for who in greeted:
        pl.semaphore_signal(barrier, inc=1, device_id=who, device_id_type=MESH)

    load_taps.wait()
    load_lag.wait()
    taps = jnp.concatenate([taps_ref[...].astype(F32).reshape(1, TAPS), jnp.zeros((1, 256 - TAPS), F32)], 1)
    banded = pltpu.roll(jnp.broadcast_to(taps, (BLOCK + TAPS, 256)), 256 - TAPS, 1, stride=1, stride_axis=0)
    toeplitz = banded[:, 0:BLOCK].T.astype(BF16)
    load.wait()

    def fir(block):
        start = block * BLOCK
        window = ext[start + GAUGE_MAX:start + GAUGE_MAX + BLOCK + TAPS]
        filtered[start + GAUGE_MAX:start + GAUGE_MAX + BLOCK] = dot(toeplitz, window)

    masks = []
    for tile in range(n_tiles):
        lag = lag_ref[tile * 128:(tile + 1) * 128].reshape(1, 128) - 1
        masks.append([lax.rem(lag // (2**b), 2) == 1 for b in range(4)])

    rows = BLOCK + GAUGE_MAX

    def difference(block):
        start = pl.multiple_of(block * BLOCK, BLOCK)
        for tile in range(n_tiles):
            cols = slice(tile * 128, (tile + 1) * 128)
            x = filtered[pl.ds(start, rows), cols]
            y = pltpu.roll(x, 1, 0)
            for b in (3, 2, 1, 0):
                y = jnp.where(jnp.broadcast_to(masks[tile][b], (rows, 128)), pltpu.roll(y, 2**b, 0), y)
            strain[pl.ds(start, BLOCK), cols] = (x - y)[GAUGE_MAX:].astype(BF16)

    for block in range(1, n_blocks):
        fir(block)

    @pl.loop(2, n_blocks)
    def _(block):
        difference(block)

    pl.semaphore_wait(barrier, len(greeted))
    halo = pltpu.make_async_remote_copy(
        src_ref=record.at[pl.ds(n_rows - HALO, HALO)], dst_ref=ext.at[pl.ds(0, HALO)],
        send_sem=halo_sem.at[0], recv_sem=halo_sem.at[1], device_id={"tm": nxt}, device_id_type=MESH)
    halo.start()
    load_proj.wait()
    late = 2 * BLOCK
    stk[0] = dot(proj_ref[late:], strain[late:], TN)
    load_comp.wait()
    comp = comp_ref[...].T
    comp_t[0] = comp
    comp_t[1, :, 0:RANK] = comp[:, RANK:]
    comp_t[1, :, RANK:] = comp[:, :RANK]
    halo.wait()
    ext[pl.ds(0, HALO)] = jnp.where(tm == 0, jnp.zeros((HALO, n_cols), BF16), ext[pl.ds(0, HALO)])
    filtered[pl.ds(0, GAUGE_MAX)] = dot(toeplitz[:GAUGE_MAX, :HALO], ext[pl.ds(0, HALO)])
    fir(0)

    @pl.loop(0, 2)
    def _(block):
        difference(block)

    stk[0] += dot(proj_ref[0:late], strain[0:late], TN)

    def remote(src, dst, send_sem, recv_sem, who):
        copy = pltpu.make_async_remote_copy(
            src_ref=src, dst_ref=dst, send_sem=send_sem, recv_sem=recv_sem, device_id=who, device_id_type=MESH)
        copy.start()
        return copy

    def send_diag(level):
        return remote(diag.at[level, 0], diag.at[level, 1], dg_sem.at[0, level], dg_sem.at[1, level],
                      {"tm": partners[level]})

    def scatter(j, value):
        part[j] = value.reshape(n_chan, slice_rows, RANK)
        scat[j, me] = part[j, me]
        copies = []
        for o in offsets:
            peer = lax.rem(me + o, n_chan)
            copies.append(remote(part.at[j, peer], scat.at[j, me], rs_send.at[j, o], rs_recv.at[j, o], {"chan": peer}))
        return copies

    def gather(j, copies):
        for copy in copies:
            copy.wait()
        gath[j, me] = jnp.sum(scat[j], axis=0)
        copies = []
        for o in offsets:
            peer = lax.rem(me + o, n_chan)
            copies.append(remote(gath.at[j, me], gath.at[j, me], ag_send.at[j, o], ag_recv.at[j, o], {"chan": peer}))
        return copies

    def finish(j, copies):
        for copy in copies:
            copy.wait()
        return gath[j].reshape(RANK, RANK)

    eye = (lax.broadcasted_iota(jnp.int32, (2 * RANK, 2 * RANK), 0)
           == lax.broadcasted_iota(jnp.int32, (2 * RANK, 2 * RANK), 1)).astype(F32)

    def split_rows(level):
        high, rest = split(stk[level])
        stk_hi[level, 0:RANK] = high
        stk_lo[level, 0:RANK] = rest
        return high, rest

    def send_rows(level, high, rest, where):
        who = {"tm": partners[level]}
        return (remote(high, stk_hi.at[level, where], ex_sem.at[0, level], ex_sem.at[1, level], who),
                remote(rest, stk_lo.at[level, where], ex_sem.at[2, level], ex_sem.at[3, level], who))

    def cross_rows(received, own):
        return dot(received, own[0], NT) + dot(received, own[1], NT)

    for level in range(levels):
        count = min(2**level, most)
        r = RANK // count
        h = r // 2
        last = level == levels - 1
        place = lax.rem(tm, count)
        got_rows = pl.ds(pl.multiple_of(RANK + place * r, 16), r)
        own = split_rows(level)
        if level == 0:
            upper_half = pl.ds(RANK, RANK)
            moving, moving_low = send_rows(0, stk_hi.at[0, pl.ds(0, RANK)], stk_lo.at[0, pl.ds(0, RANK)], upper_half)
        if level == 0:
            diag_moving = scatter(0, dot3(own, own, NT))
            diag_moving = gather(0, diag_moving)
            moving.wait()
            cross_moving = scatter(1, cross_rows(stk_hi[0, RANK:], own))
            moving_low.wait()
            diag[0, 0] = finish(0, diag_moving)
            diag_copy = send_diag(0)
            cross_moving = gather(1, cross_moving)
            below = finish(1, cross_moving)
        else:
            mix = (mix_hi[...], mix_lo[...])
            diag[level, 0] = dot3(split(dot3(mix, split(gram[...]))), mix, NT)
            diag_copy = send_diag(level)
            moving.wait()
            direct = h == 8
            align = min(h, 16)
            value = cross_rows(stk_hi[level, got_rows], own)
            crossp[level, 0:r] = value
            if not direct:
                crossp_b[level, 0:r] = value.astype(BF16)
            half = pl.ds(pl.multiple_of(core * h, align), h)
            away = pl.ds(pl.multiple_of((1 - core) * h, align), h)
            if direct:
                peers = []
                for o in offsets:
                    peer = lax.rem(me + o, n_chan)
                    rows_there = pl.ds(pl.multiple_of(lax.rem(peer, 2) * h, 8), h)
                    peers.append(remote(crossp.at[level, rows_there], wide.at[level, me],
                                        w_send.at[level, o], w_recv.at[level, o], {"chan": peer}))
                wide[level, me] = crossp[level, half]
            else:
                pre_copy = remote(crossp_b.at[level, away], pre.at[level, pl.ds(0, h)],
                                  pre_sem.at[0, level], pre_sem.at[1, level], {"chan": other_core})
            forwards = []
            moving_low.wait()
            for i in range(1, count):
                for k, side in enumerate((stk_hi, stk_lo)):
                    forwards.append(remote(side.at[level, got_rows], side.at[level, got_rows],
                                           f_send.at[level, 2 * i + k], f_recv.at[level, 2 * i + k],
                                           {"tm": member(count, i)}))
            if direct:
                for copy in peers:
                    copy.wait()
                total = jnp.sum(wide[level], axis=0)
            else:
                pre_copy.wait()
                slot = zbuf.at[level, z_me, pl.ds(0, h)]
                slot[...] = (crossp[level, half] + pre[level, 0:h].astype(F32)).astype(BF16)
                copies = []
                for o in z_offsets:
                    peer = lax.rem(me + 2 * o, n_chan)
                    copies.append(remote(slot, slot, z_send.at[level, o], z_recv.at[level, o], {"chan": peer}))
                for copy in copies:
                    copy.wait()
                total = jnp.sum(zbuf[level, :, 0:h].astype(F32), axis=0)
            joined = cross if direct else cross_b
            chunk = joined.at[level, pl.ds(pl.multiple_of(place * r + core * h, align), h)]
            chunk[...] = total.astype(chunk.dtype)
            copies = []
            for i in range(count - 1, -1, -1):
                for d in range(2):
                    if i + d > 0:
                        who = {"tm": member(count, i), "chan": me if d == 0 else other_core}
                        copies.append(remote(chunk, chunk, g_send.at[level, 2 * i + d], g_recv.at[level, 2 * i + d], who))
            for copy in forwards:
                copy.wait()
            for copy in copies:
                copy.wait()
            below = joined[level].astype(F32)

        gram[RANK:, 0:RANK] = below
        gram[0:RANK, RANK:] = below.T
        gram[0:RANK, 0:RANK] = diag[level, 0]
        diag_copy.wait()
        gram[RANK:, RANK:] = diag[level, 1]

        value = gram[...]
        mean = jnp.sum(value * eye, keepdims=True) / (2 * RANK)
        shifted = value - mean * eye
        z = shifted / jnp.sqrt(jnp.sum(shifted * shifted, keepdims=True) + 1e-06)
        for step in range(K_ITERS):
            if step < COARSE:
                rounded = z.astype(BF16)
                z = 1.5 * z - 0.5 * dot(rounded, dot(rounded, rounded).astype(BF16))
                continue
            parts = split(z)
            z = 1.5 * z - 0.5 * dot3(parts, split(dot3(parts, parts)))

        upper = lax.rem(tm // 2**level, 2)
        parts = split(z)
        both = (stk_hi[level], stk_lo[level])

        def mixed(rows):
            mine = comp_t[upper, rows]
            return split(0.5 * (mine + dot3(split(mine), parts)))

        if not last:
            after = min(2 * 2**level, most)
            size = RANK // after
            spot = lax.rem(tm, after) * size
            early, early_low = split(dot3(mixed(pl.ds(pl.multiple_of(spot, 16), size)), both))
            ahead_hi[level + 1, 0:size] = early
            ahead_lo[level + 1, 0:size] = early_low
            moving, moving_low = send_rows(level + 1, ahead_hi.at[level + 1, pl.ds(0, size)],
                                           ahead_lo.at[level + 1, pl.ds(0, size)],
                                           pl.ds(pl.multiple_of(RANK + spot, 16), size))
            mix = mixed(pl.ds(0, RANK))
            mix_hi[...], mix_lo[...] = mix
            stk[level + 1] = dot3(mix, both)
        else:
            share = RANK // n_tm
            group = max(8, share)
            result = dot3(mixed(pl.ds(pl.multiple_of(tm * share // group * group, 8), group)), both)
            spot = lax.rem(tm, group // share)
            chosen = result[0:share]
            for i in range(1, group // share):
                chosen = jnp.where(spot == i, result[i * share:(i + 1) * share], chosen)
            out_ref[...] = chosen


def on_device(n_tm, n_chan, record, fir_taps, gauge_lag, projector, compress):
    n_rows, n_cols = record.shape
    levels = n_tm.bit_length() - 1
    slice_rows = RANK // n_chan
    most = min(MOST, n_tm)
    dma = pltpu.SemaphoreType.DMA
    vmem = pl.BlockSpec(memory_space=pltpu.VMEM)
    hbm = pl.BlockSpec(memory_space=pltpu.HBM)
    return pl.pallas_call(
        functools.partial(kernel, n_tm, n_chan, levels),
        out_shape=jax.ShapeDtypeStruct((RANK // n_tm, n_cols), F32),
        in_specs=[hbm] * 5,
        out_specs=vmem,
        scratch_shapes=[
            pltpu.VMEM((HALO + n_rows, n_cols), BF16),
            pltpu.VMEM((GAUGE_MAX + n_rows, n_cols), F32),
            pltpu.VMEM((n_rows, n_cols), BF16),
            pltpu.VMEM((n_rows, RANK), BF16),
            pltpu.VMEM((2 * RANK, RANK), F32),
            pltpu.VMEM((TAPS,), BF16),
            pltpu.VMEM((n_cols,), jnp.int32),
            pltpu.VMEM((levels, RANK, n_cols), F32),
            pltpu.VMEM((levels, 2 * RANK, n_cols), BF16),
            pltpu.VMEM((levels, 2 * RANK, n_cols), BF16),
            pltpu.VMEM((2 * RANK, 2 * RANK), F32),
            pltpu.VMEM((levels, 2, RANK, RANK), F32),
            pltpu.VMEM((2, RANK, 2 * RANK), F32),
            pltpu.VMEM((2, n_chan, slice_rows, RANK), F32),
            pltpu.VMEM((2, n_chan, slice_rows, RANK), F32),
            pltpu.VMEM((2, n_chan, slice_rows, RANK), F32),
            pltpu.VMEM((levels, RANK // 2, RANK), F32),
            pltpu.VMEM((levels, RANK // 2, RANK), BF16),
            pltpu.VMEM((levels, RANK // 4, RANK), BF16),
            pltpu.VMEM((levels, n_chan // 2, RANK // 4, RANK), BF16),
            pltpu.VMEM((levels, n_chan, 8, RANK), F32),
            pltpu.VMEM((levels, RANK, RANK), F32),
            pltpu.VMEM((levels, RANK, RANK), BF16),
            pltpu.VMEM((levels, RANK // 2, n_cols), BF16),
            pltpu.VMEM((levels, RANK // 2, n_cols), BF16),
            pltpu.VMEM((RANK, 2 * RANK), BF16),
            pltpu.VMEM((RANK, 2 * RANK), BF16),
            dma((5,)),
            dma((2,)),
            dma((4, levels)),
            dma((2, levels)),
            dma((2, n_chan)),
            dma((2, n_chan)),
            dma((2, n_chan)),
            dma((2, n_chan)),
            dma((2, levels)),
            dma((levels, n_chan // 2)),
            dma((levels, n_chan // 2)),
            dma((levels, 2 * most)),
            dma((levels, 2 * most)),
            dma((levels, 2 * most)),
            dma((levels, 2 * most)),
            dma((levels, n_chan)),
            dma((levels, n_chan)),
        ],
        compiler_params=pltpu.CompilerParams(collective_id=0, has_side_effects=True, vmem_limit_bytes=67_000_000),
    )(record, fir_taps, gauge_lag, projector, compress)


def solution(mesh):
    return jax.shard_map(
        functools.partial(on_device, mesh.shape["tm"], mesh.shape["chan"]),
        mesh=mesh,
        in_specs=(P("tm", "chan"), P(), P("chan"), P("tm", None), P()),
        out_specs=P("tm", "chan"),
        check_vma=False,
    )
```

```python
import functools

import jax
import jax.numpy as jnp
from jax import lax
from jax.experimental import pallas as pl
from jax.experimental.pallas import tpu as pltpu
from jax.sharding import PartitionSpec as P

TAPS = 64
GAUGE_MAX = 16
K_ITERS = 8
HALO = 80
RANK = 128
BLOCK = 128
MOST = 8
COARSE = 7
MESH = pl.DeviceIdType.MESH
F32 = jnp.float32
BF16 = jnp.bfloat16


def split(value):
    high = value.astype(BF16)
    return high, (value - high.astype(F32)).astype(BF16)


def dot(first, second, contract=((1,), (0,))):
    return lax.dot_general(first, second, (contract, ((), ())), preferred_element_type=F32)


def dot3(first, second, contract=((1,), (0,))):
    fh, fl = first
    sh, sl = second
    return dot(fh, sh, contract) + (dot(fh, sl, contract) + dot(fl, sh, contract))


NT = ((1,), (1,))
TN = ((0,), (0,))


def kernel(n_tm, n_chan, levels, record, taps_hbm, lag_hbm, proj_hbm, comp_hbm, out_ref,
           ext, filtered, strain, proj_ref, comp_ref, taps_ref, lag_ref, stk, stk_hi, stk_lo, gram, diag, comp_t, part, scat, gath,
           crossp, crossp_b, pre, zbuf, wide, cross, cross_b, ahead_hi, ahead_lo, mix_hi, mix_lo,
           local_sem, halo_sem, ex_sem, dg_sem, rs_send, rs_recv, ag_send, ag_recv,
           pre_sem, z_send, z_recv, g_send, g_recv, f_send, f_recv, w_send, w_recv):
    tm = lax.axis_index("tm")
    me = lax.axis_index("chan")
    n_rows, n_cols = record.shape
    slice_rows = RANK // n_chan
    n_blocks = n_rows // BLOCK
    n_tiles = n_cols // 128
    n_z = n_chan // 2
    core = lax.rem(me, 2)
    z_me = me // 2
    other_core = me + 1 - 2 * core

    load = pltpu.make_async_copy(record, ext.at[pl.ds(HALO, n_rows)], local_sem.at[0])
    load_proj = pltpu.make_async_copy(proj_hbm, proj_ref, local_sem.at[1])
    load_comp = pltpu.make_async_copy(comp_hbm, comp_ref, local_sem.at[2])
    load_taps = pltpu.make_async_copy(taps_hbm, taps_ref, local_sem.at[3])
    load_lag = pltpu.make_async_copy(lag_hbm, lag_ref, local_sem.at[4])
    load_taps.start()
    load_lag.start()
    load.start()
    load_proj.start()
    load_comp.start()

    nxt = lax.rem(tm + 1, n_tm)
    prv = lax.rem(tm + n_tm - 1, n_tm)
    partners = []
    for level in range(levels):
        bit = 2**level
        partners.append(tm + bit * (1 - 2 * lax.rem(tm // bit, 2)))
    offsets = sorted(range(1, n_chan), key=lambda o: -min(o, n_chan - o))
    z_offsets = sorted(range(1, n_z), key=lambda o: -min(o, n_z - o))
    most = min(MOST, n_tm)

    def member(count, i):
        return tm // count * count + lax.rem(tm + i, count)

    barrier = pltpu.get_barrier_semaphore()
    greeted = [{"tm": nxt}, {"tm": prv}]
    greeted += [{"tm": partners[level]} for level in range(levels) if 2**level >= most]
    greeted += [{"chan": lax.rem(me + o, n_chan)} for o in offsets]
    greeted += [{"tm": member(most, i), "chan": c} for i in range(1, most) for c in (me, other_core)]
    for who in greeted:
        pl.semaphore_signal(barrier, inc=1, device_id=who, device_id_type=MESH)

    load_taps.wait()
    load_lag.wait()
    taps = jnp.concatenate([taps_ref[...].astype(F32).reshape(1, TAPS), jnp.zeros((1, 256 - TAPS), F32)], 1)
    banded = pltpu.roll(jnp.broadcast_to(taps, (BLOCK + TAPS, 256)), 256 - TAPS, 1, stride=1, stride_axis=0)
    toeplitz = banded[:, 0:BLOCK].T.astype(BF16)
    load.wait()

    def fir(block):
        start = block * BLOCK
        window = ext[start + GAUGE_MAX:start + GAUGE_MAX + BLOCK + TAPS]
        filtered[start + GAUGE_MAX:start + GAUGE_MAX + BLOCK] = dot(toeplitz, window)

    masks = []
    for tile in range(n_tiles):
        lag = lag_ref[tile * 128:(tile + 1) * 128].reshape(1, 128) - 1
        masks.append([lax.rem(lag // (2**b), 2) == 1 for b in range(4)])

    rows = BLOCK + GAUGE_MAX

    def difference(block):
        start = pl.multiple_of(block * BLOCK, BLOCK)
        for tile in range(n_tiles):
            cols = slice(tile * 128, (tile + 1) * 128)
            x = filtered[pl.ds(start, rows), cols]
            y = pltpu.roll(x, 1, 0)
            for b in (3, 2, 1, 0):
                y = jnp.where(jnp.broadcast_to(masks[tile][b], (rows, 128)), pltpu.roll(y, 2**b, 0), y)
            strain[pl.ds(start, BLOCK), cols] = (x - y)[GAUGE_MAX:].astype(BF16)

    for block in range(1, n_blocks):
        fir(block)

    @pl.loop(2, n_blocks)
    def _(block):
        difference(block)

    pl.semaphore_wait(barrier, len(greeted))
    halo = pltpu.make_async_remote_copy(
        src_ref=record.at[pl.ds(n_rows - HALO, HALO)], dst_ref=ext.at[pl.ds(0, HALO)],
        send_sem=halo_sem.at[0], recv_sem=halo_sem.at[1], device_id={"tm": nxt}, device_id_type=MESH)
    halo.start()
    load_proj.wait()
    late = 2 * BLOCK
    stk[0] = dot(proj_ref[late:], strain[late:], TN)
    load_comp.wait()
    comp = comp_ref[...].T
    comp_t[0] = comp
    comp_t[1, :, 0:RANK] = comp[:, RANK:]
    comp_t[1, :, RANK:] = comp[:, :RANK]
    halo.wait()
    ext[pl.ds(0, HALO)] = jnp.where(tm == 0, jnp.zeros((HALO, n_cols), BF16), ext[pl.ds(0, HALO)])
    filtered[pl.ds(0, GAUGE_MAX)] = dot(toeplitz[:GAUGE_MAX, :HALO], ext[pl.ds(0, HALO)])
    fir(0)

    @pl.loop(0, 2)
    def _(block):
        difference(block)

    stk[0] += dot(proj_ref[0:late], strain[0:late], TN)

    def remote(src, dst, send_sem, recv_sem, who):
        copy = pltpu.make_async_remote_copy(
            src_ref=src, dst_ref=dst, send_sem=send_sem, recv_sem=recv_sem, device_id=who, device_id_type=MESH)
        copy.start()
        return copy

    def send_diag(level):
        return remote(diag.at[level, 0], diag.at[level, 1], dg_sem.at[0, level], dg_sem.at[1, level],
                      {"tm": partners[level]})

    def scatter(j, value):
        part[j] = value.reshape(n_chan, slice_rows, RANK)
        scat[j, me] = part[j, me]
        copies = []
        for o in offsets:
            peer = lax.rem(me + o, n_chan)
            copies.append(remote(part.at[j, peer], scat.at[j, me], rs_send.at[j, o], rs_recv.at[j, o], {"chan": peer}))
        return copies

    def gather(j, copies):
        for copy in copies:
            copy.wait()
        gath[j, me] = jnp.sum(scat[j], axis=0)
        copies = []
        for o in offsets:
            peer = lax.rem(me + o, n_chan)
            copies.append(remote(gath.at[j, me], gath.at[j, me], ag_send.at[j, o], ag_recv.at[j, o], {"chan": peer}))
        return copies

    def finish(j, copies):
        for copy in copies:
            copy.wait()
        return gath[j].reshape(RANK, RANK)

    eye = (lax.broadcasted_iota(jnp.int32, (2 * RANK, 2 * RANK), 0)
           == lax.broadcasted_iota(jnp.int32, (2 * RANK, 2 * RANK), 1)).astype(F32)

    def split_rows(level):
        high, rest = split(stk[level])
        stk_hi[level, 0:RANK] = high
        stk_lo[level, 0:RANK] = rest
        return high, rest

    def send_rows(level, high, rest, where):
        who = {"tm": partners[level]}
        return (remote(high, stk_hi.at[level, where], ex_sem.at[0, level], ex_sem.at[1, level], who),
                remote(rest, stk_lo.at[level, where], ex_sem.at[2, level], ex_sem.at[3, level], who))

    def cross_rows(received, own):
        return dot(received, own[0], NT) + dot(received, own[1], NT)

    for level in range(levels):
        count = min(2**level, most)
        r = RANK // count
        h = r // 2
        last = level == levels - 1
        place = lax.rem(tm, count)
        got_rows = pl.ds(pl.multiple_of(RANK + place * r, 16), r)
        own = split_rows(level)
        if level == 0:
            upper_half = pl.ds(RANK, RANK)
            moving, moving_low = send_rows(0, stk_hi.at[0, pl.ds(0, RANK)], stk_lo.at[0, pl.ds(0, RANK)], upper_half)
        if level == 0:
            diag_moving = scatter(0, dot3(own, own, NT))
            diag_moving = gather(0, diag_moving)
            moving.wait()
            cross_moving = scatter(1, cross_rows(stk_hi[0, RANK:], own))
            moving_low.wait()
            diag[0, 0] = finish(0, diag_moving)
            diag_copy = send_diag(0)
            cross_moving = gather(1, cross_moving)
            below = finish(1, cross_moving)
        else:
            mix = (mix_hi[...], mix_lo[...])
            diag[level, 0] = dot3(split(dot3(mix, split(gram[...]))), mix, NT)
            diag_copy = send_diag(level)
            moving.wait()
            direct = h == 8
            align = min(h, 16)
            value = cross_rows(stk_hi[level, got_rows], own)
            crossp[level, 0:r] = value
            if not direct:
                crossp_b[level, 0:r] = value.astype(BF16)
            half = pl.ds(pl.multiple_of(core * h, align), h)
            away = pl.ds(pl.multiple_of((1 - core) * h, align), h)
            if direct:
                peers = []
                for o in offsets:
                    peer = lax.rem(me + o, n_chan)
                    rows_there = pl.ds(pl.multiple_of(lax.rem(peer, 2) * h, 8), h)
                    peers.append(remote(crossp.at[level, rows_there], wide.at[level, me],
                                        w_send.at[level, o], w_recv.at[level, o], {"chan": peer}))
                wide[level, me] = crossp[level, half]
            else:
                pre_copy = remote(crossp_b.at[level, away], pre.at[level, pl.ds(0, h)],
                                  pre_sem.at[0, level], pre_sem.at[1, level], {"chan": other_core})
            forwards = []
            def pass_on():
                moving_low.wait()
                for i in range(1, count):
                    for k, side in enumerate((stk_hi, stk_lo)):
                        forwards.append(remote(side.at[level, got_rows], side.at[level, got_rows],
                                               f_send.at[level, 2 * i + k], f_recv.at[level, 2 * i + k],
                                               {"tm": member(count, i)}))

            if direct:
                pass_on()
                for copy in peers:
                    copy.wait()
                total = jnp.sum(wide[level], axis=0)
            else:
                pre_copy.wait()
                slot = zbuf.at[level, z_me, pl.ds(0, h)]
                slot[...] = (crossp[level, half] + pre[level, 0:h].astype(F32)).astype(BF16)
                copies = []
                for o in z_offsets:
                    peer = lax.rem(me + 2 * o, n_chan)
                    copies.append(remote(slot, slot, z_send.at[level, o], z_recv.at[level, o], {"chan": peer}))
                pass_on()
                for copy in copies:
                    copy.wait()
                total = jnp.sum(zbuf[level, :, 0:h].astype(F32), axis=0)
            joined = cross if direct else cross_b
            chunk = joined.at[level, pl.ds(pl.multiple_of(place * r + core * h, align), h)]
            chunk[...] = total.astype(chunk.dtype)
            copies = []
            for i in range(count - 1, -1, -1):
                for d in range(2):
                    if i + d > 0:
                        who = {"tm": member(count, i), "chan": me if d == 0 else other_core}
                        copies.append(remote(chunk, chunk, g_send.at[level, 2 * i + d], g_recv.at[level, 2 * i + d], who))
            for copy in forwards:
                copy.wait()
            for copy in copies:
                copy.wait()
            below = joined[level].astype(F32)

        gram[RANK:, 0:RANK] = below
        gram[0:RANK, RANK:] = below.T
        gram[0:RANK, 0:RANK] = diag[level, 0]
        diag_copy.wait()
        gram[RANK:, RANK:] = diag[level, 1]

        value = gram[...]
        mean = jnp.sum(value * eye, keepdims=True) / (2 * RANK)
        shifted = value - mean * eye
        z = shifted / jnp.sqrt(jnp.sum(shifted * shifted, keepdims=True) + 1e-06)
        for step in range(K_ITERS):
            if step < COARSE:
                rounded = z.astype(BF16)
                z = 1.5 * z - 0.5 * dot(rounded, dot(rounded, rounded).astype(BF16))
                continue
            parts = split(z)
            z = 1.5 * z - 0.5 * dot3(parts, split(dot3(parts, parts)))

        upper = lax.rem(tm // 2**level, 2)
        parts = split(z)
        both = (stk_hi[level], stk_lo[level])

        def mixed(rows):
            mine = comp_t[upper, rows]
            return split(0.5 * (mine + dot3(split(mine), parts)))

        if not last:
            after = min(2 * 2**level, most)
            size = RANK // after
            spot = lax.rem(tm, after) * size
            early, early_low = split(dot3(mixed(pl.ds(pl.multiple_of(spot, 16), size)), both))
            ahead_hi[level + 1, 0:size] = early
            ahead_lo[level + 1, 0:size] = early_low
            moving, moving_low = send_rows(level + 1, ahead_hi.at[level + 1, pl.ds(0, size)],
                                           ahead_lo.at[level + 1, pl.ds(0, size)],
                                           pl.ds(pl.multiple_of(RANK + spot, 16), size))
            mix = mixed(pl.ds(0, RANK))
            mix_hi[...], mix_lo[...] = mix
            stk[level + 1] = dot3(mix, both)
        else:
            share = RANK // n_tm
            group = max(8, share)
            result = dot3(mixed(pl.ds(pl.multiple_of(tm * share // group * group, 8), group)), both)
            spot = lax.rem(tm, group // share)
            chosen = result[0:share]
            for i in range(1, group // share):
                chosen = jnp.where(spot == i, result[i * share:(i + 1) * share], chosen)
            out_ref[...] = chosen


def on_device(n_tm, n_chan, record, fir_taps, gauge_lag, projector, compress):
    n_rows, n_cols = record.shape
    levels = n_tm.bit_length() - 1
    slice_rows = RANK // n_chan
    most = min(MOST, n_tm)
    dma = pltpu.SemaphoreType.DMA
    vmem = pl.BlockSpec(memory_space=pltpu.VMEM)
    hbm = pl.BlockSpec(memory_space=pltpu.HBM)
    return pl.pallas_call(
        functools.partial(kernel, n_tm, n_chan, levels),
        out_shape=jax.ShapeDtypeStruct((RANK // n_tm, n_cols), F32),
        in_specs=[hbm] * 5,
        out_specs=vmem,
        scratch_shapes=[
            pltpu.VMEM((HALO + n_rows, n_cols), BF16),
            pltpu.VMEM((GAUGE_MAX + n_rows, n_cols), F32),
            pltpu.VMEM((n_rows, n_cols), BF16),
            pltpu.VMEM((n_rows, RANK), BF16),
            pltpu.VMEM((2 * RANK, RANK), F32),
            pltpu.VMEM((TAPS,), BF16),
            pltpu.VMEM((n_cols,), jnp.int32),
            pltpu.VMEM((levels, RANK, n_cols), F32),
            pltpu.VMEM((levels, 2 * RANK, n_cols), BF16),
            pltpu.VMEM((levels, 2 * RANK, n_cols), BF16),
            pltpu.VMEM((2 * RANK, 2 * RANK), F32),
            pltpu.VMEM((levels, 2, RANK, RANK), F32),
            pltpu.VMEM((2, RANK, 2 * RANK), F32),
            pltpu.VMEM((2, n_chan, slice_rows, RANK), F32),
            pltpu.VMEM((2, n_chan, slice_rows, RANK), F32),
            pltpu.VMEM((2, n_chan, slice_rows, RANK), F32),
            pltpu.VMEM((levels, RANK // 2, RANK), F32),
            pltpu.VMEM((levels, RANK // 2, RANK), BF16),
            pltpu.VMEM((levels, RANK // 4, RANK), BF16),
            pltpu.VMEM((levels, n_chan // 2, RANK // 4, RANK), BF16),
            pltpu.VMEM((levels, n_chan, 8, RANK), F32),
            pltpu.VMEM((levels, RANK, RANK), F32),
            pltpu.VMEM((levels, RANK, RANK), BF16),
            pltpu.VMEM((levels, RANK // 2, n_cols), BF16),
            pltpu.VMEM((levels, RANK // 2, n_cols), BF16),
            pltpu.VMEM((RANK, 2 * RANK), BF16),
            pltpu.VMEM((RANK, 2 * RANK), BF16),
            dma((5,)),
            dma((2,)),
            dma((4, levels)),
            dma((2, levels)),
            dma((2, n_chan)),
            dma((2, n_chan)),
            dma((2, n_chan)),
            dma((2, n_chan)),
            dma((2, levels)),
            dma((levels, n_chan // 2)),
            dma((levels, n_chan // 2)),
            dma((levels, 2 * most)),
            dma((levels, 2 * most)),
            dma((levels, 2 * most)),
            dma((levels, 2 * most)),
            dma((levels, n_chan)),
            dma((levels, n_chan)),
        ],
        compiler_params=pltpu.CompilerParams(collective_id=0, has_side_effects=True, vmem_limit_bytes=67_000_000),
    )(record, fir_taps, gauge_lag, projector, compress)


def solution(mesh):
    return jax.shard_map(
        functools.partial(on_device, mesh.shape["tm"], mesh.shape["chan"]),
        mesh=mesh,
        in_specs=(P("tm", "chan"), P(), P("chan"), P("tm", None), P()),
        out_specs=P("tm", "chan"),
        check_vma=False,
    )
```
